512 devices in a mesh: dp: 32 (over x, y), table: 16 (over z, core).
Axes of the slice: x: 4, y: 8, z: 8, core: 2. Of those that a mesh axis runs over, the one named last changes fastest.
Arguments:
- table: bfloat16 [12288, 512], P('table'), may hold values from -6 to 6
- history_shard: int32 [512, 256, 1], P(('dp', 'table')), may hold values from 0 to 15; in each aligned block of 256 rows (0 to 255, 256 to 511, ..., all dimensions but the last counted through in order) at most 32 rows name the same one
- history_row: int32 [512, 256], P(('dp', 'table')), may hold values from 0 to 767
- lengths: int32 [512], P(('dp', 'table')), may hold values from 1 to 256, 98304 in all
- w_in: bfloat16 [512, 2048], replicated, may hold values from -0.25 to 0.25
- w_out: bfloat16 [512, 512], replicated, may hold values from -0.25 to 0.25
- cotangent: bfloat16 [512, 256, 512], P(('dp', 'table')), may hold values from -6 to 6
Outputs:
- table_grad: float32 [12288, 512], P('table')
- dense_grad: bfloat16 [512, 512], replicated
The draws below stay inside these ranges and needn't reach their ends.
Inputs may be any that keep to these rules, and one draw needn't show every extreme that they name: `history_shard`: among the 256 history slots of one device's samples, at most 32 name one table shard, and that bound is met by some shard in some device's slots. `lengths`: some sample has the full length 256.
All inputs are finite; a program needn't handle non-finite values. No bound on the sum of `lengths` on one device may be relied on, other than what follows from the above.
Results may differ from the reference program's by a relative error of at most 0.017.
Values may be sent and summed in bfloat16 or wider, within the bound.
A program may use at most 64 MiB of HBM per device.

```python
import math
import jax
import jax.numpy as jnp
import numpy as np
from jax import lax

E = 512
HEADS = 4
LMAX = 256
B_DEV = 1
V_DEV = 768
SAMPLES = 512
VOCAB = 12288
CAP = 32
N_TABLE = 16


def with_ends(values, key, smallest, largest):
    dims = values.shape
    spot = [jax.random.randint(jax.random.fold_in(key, axis), (), 0, dims[axis]) for axis in range(len(dims))]
    values = values.at[tuple(spot)].set(smallest)
    longest = dims.index(max(dims))
    spot[longest] = (spot[longest] + 1) % dims[longest]
    return values.at[tuple(spot)].set(largest)


def with_spikes(entries, key, source, target, blocks, factor):
    def block_of(position):
        return (jnp.arange(entries.shape[position]) // (entries.shape[position] // blocks)).reshape((-1,) + (1,) * (entries.ndim - 1 - position))

    near = jax.random.permutation(key, blocks)[block_of(target)]
    second = (block_of(target) + blocks // 2) % blocks
    return jnp.where((block_of(source) == near) | (block_of(source) == second), factor * entries, entries)


def block_scale(stream_key, dims, split, least, top_value):
    level = 1.0
    for axis_at, shards_of in split:
        heights = jax.random.uniform(jax.random.fold_in(jax.random.fold_in(stream_key, 6), axis_at), (shards_of,), jnp.float32, least / len(split), top_value / len(split))
        level = level * jnp.repeat(jnp.exp(heights), dims[axis_at] // shards_of).reshape((-1,) + (1,) * (len(dims) - 1 - axis_at))
    return level


def profile(number_of, total, bound, slope):
    weights = [(1 << 20) // math.isqrt(rank ** slope) + 1 for rank in range(2, number_of + 1)]
    surplus, given = total - bound - (number_of - 1), [1] * (number_of - 1)
    while surplus > 0:
        free = [i for i in range(number_of - 1) if given[i] < bound]
        pool, left = sum([weights[i] for i in free]), surplus
        for i in free:
            extra = min(bound - given[i], max(1, left * weights[i] // pool), surplus)
            given[i] = given[i] + extra
            surplus = surplus - extra
    return np.array([bound] + given)


def uneven_parts(rng, number_of, total, limit, lean):
    if number_of == 2:
        one = jax.random.randint(rng, (), max(1, total - limit), min(limit, total - 1) + 1)
        return jnp.stack([one, total - one])
    sizes = jnp.asarray(profile(number_of, total, limit, lean), jnp.int32)
    pairs = (number_of - 1) // 2
    donor, sink = sizes[1:1 + 2 * pairs:2], sizes[2:2 + 2 * pairs:2]
    slack = jnp.minimum(donor - 1, limit - sink)
    shifted = jax.random.randint(jax.random.fold_in(rng, 1), (pairs,), 0, 1 << 20) % (slack + 1)
    sizes = sizes.at[1:1 + 2 * pairs:2].set(donor - shifted).at[2:2 + 2 * pairs:2].set(sink + shifted)
    return sizes[jax.random.permutation(jax.random.fold_in(rng, 2), number_of)]


def assign_block(rng, own, number, rows, amount, top, reach, skew):
    sequence = jax.random.permutation(rng, amount)
    packed, ordinary = portions_of(amount, rows * top, reach, skew, True), portions_of(amount, rows * top, reach, skew, False)
    places = jnp.arange(amount)

    def named(tallies, offset_by):
        used = int((tallies > 0).sum())
        fixed = max(1, used // 4)
        moved = fixed + (places - fixed + offset_by * (used - fixed)) % max(1, amount - fixed)
        return jnp.zeros((amount,), jnp.int32).at[sequence[jnp.where(places < fixed, places, moved)]].set(jnp.asarray(tallies, jnp.int32))

    tallies = jnp.where(number % 4 == 0, named(packed, number // 4), named(ordinary, number - number // 4 - 1))
    mixed = jax.random.permutation(jax.random.fold_in(own, 3), amount)
    giver, sink = mixed[0:amount // 2 * 2:2], mixed[1:amount // 2 * 2:2]
    slack = jnp.minimum(tallies[giver] - 1, reach - tallies[sink]) // 2
    slack = jnp.where((giver == sequence[0]) | (sink == sequence[0]) | (tallies[sink] == 0), 0, jnp.maximum(slack, 0))
    moved = jax.random.randint(jax.random.fold_in(own, 4), (amount // 2,), 0, 1 << 20) % (slack + 1)
    tallies = tallies.at[giver].add(-moved).at[sink].add(moved)
    members = jnp.searchsorted(jnp.cumsum(tallies), jnp.arange(rows * top), side="right").astype(jnp.int32)
    table = members.reshape(top, rows).T
    table = table[jax.random.permutation(jax.random.fold_in(own, 1), rows)]
    offset_by = jax.random.randint(jax.random.fold_in(own, 2), (rows, 1), 0, top)
    return jnp.take_along_axis(table, (jnp.arange(top)[None, :] + offset_by) % top, axis=1)


def portions_of(count, total, bound, skew, full):
    weights = [(1 << 20) // math.isqrt(standing ** skew) + 1 for standing in range(1, count + 1)]
    largest = bound if full else min(bound, max(-(-total // count), total * weights[0] // sum(weights)))
    least = 1 if total - largest >= count - 1 else 0
    given, surplus = [largest] + [least] * (count - 1), total - largest - least * (count - 1)
    while surplus > 0:
        movable = [i for i in range(1, count) if given[i] < largest] or [i for i in range(1, count) if given[i] < bound]
        whole, remaining = sum([weights[i] for i in movable]), surplus
        for i in movable:
            extra = min(bound - given[i], max(1, remaining * weights[i] // whole), surplus)
            given[i] = given[i] + extra
            surplus = surplus - extra
    return np.array(given)


def bell_draw(key, extent, width, most, cuts=(), held_as=jnp.bfloat16):
    array = width * jax.random.normal(key, extent, jnp.float32)
    if cuts:
        array = array * block_scale(key, extent, cuts, -0.22, 0.18)
    return jnp.clip(array, -most, most).astype(held_as)


def gaussian_with(key, shape, deviation, most, split, heavy, held_as=jnp.bfloat16):
    array = deviation * jax.random.normal(key, shape, jnp.float32)
    if split:
        array = array * block_scale(key, shape, split, -0.22, 0.18)
    return jnp.clip(with_spikes(array, jax.random.fold_in(key, 3), *heavy), -most, most).astype(held_as)


def setup_inputs(seed: int = 0) -> dict:
    key_list = jax.random.split(jax.random.key(seed), 8)
    table = bell_draw(key_list[0], (VOCAB, E), 1.0, 6.0, ((0, 16),))
    history_shard_keys = jax.random.split(jax.random.fold_in(key_list[1], 1), SAMPLES * LMAX // (B_DEV * LMAX))
    history_shard_turns = jax.random.permutation(jax.random.fold_in(key_list[1], 3), SAMPLES * LMAX // (B_DEV * LMAX))
    history_shard = jax.vmap(lambda own, number: assign_block(jax.random.fold_in(key_list[1], 2), own, number, B_DEV * LMAX, N_TABLE, 1, CAP, 2))(history_shard_keys, history_shard_turns).reshape((SAMPLES, LMAX, 1))
    history_row = with_ends(jax.random.randint(key_list[2], (SAMPLES, LMAX), 0, V_DEV), jax.random.fold_in(key_list[2], 1), 0, V_DEV - 1).astype(jnp.int32)
    lengths = uneven_parts(key_list[3], SAMPLES, 3 * SAMPLES * LMAX // 4, LMAX, 2).astype(jnp.int32)
    w_in = bell_draw(key_list[4], (E, 4 * E), E ** -0.5, 0.25)
    w_out = bell_draw(key_list[5], (E, E), E ** -0.5, 0.25)
    cotangent = gaussian_with(key_list[6], (SAMPLES, LMAX, E), 0.25, 6.0, ((0, 512),), (0, 2, 512, 6.0))
    return {"table": table, "history_shard": history_shard, "history_row": history_row, "lengths": lengths, "w_in": w_in, "w_out": w_out, "cotangent": cotangent}


def layer_norm(values):
    average = lax.optimization_barrier(jnp.mean(values, axis=-1, keepdims=True))
    centred = values - average
    variance = lax.optimization_barrier(jnp.mean(centred * centred, axis=-1, keepdims=True))
    return centred * lax.rsqrt(variance + 1e-06)

def hstu_layer(embedded, w_in, w_out, lengths):
    samples_here, seq_span, model_width = embedded.shape
    head_dim = model_width // HEADS
    normed = layer_norm(embedded.astype(jnp.float32)).astype(jnp.bfloat16)
    projected = jax.nn.silu(jnp.dot(normed.reshape(samples_here * seq_span, model_width), w_in, preferred_element_type=jnp.float32))
    gate_part = projected[:, :model_width]
    shaped = (samples_here, seq_span, HEADS, head_dim)
    values = projected[:, model_width:2 * model_width].astype(jnp.bfloat16).reshape(shaped)
    queries = projected[:, 2 * model_width:3 * model_width].astype(jnp.bfloat16).reshape(shaped)
    keys = projected[:, 3 * model_width:].astype(jnp.bfloat16).reshape(shaped)
    scores = jnp.einsum('blhd,bmhd->bhlm', queries.astype(jnp.float32), keys.astype(jnp.float32)) * head_dim ** (-0.5)
    positions = jnp.arange(seq_span)
    live_keys = (positions[None, None, :] <= positions[None, :, None]) & (positions[None, None, :] < lengths[:, None, None])
    weights = jnp.where(live_keys[:, None], jax.nn.silu(scores), 0.0) / lengths.astype(jnp.float32)[:, None, None, None]
    weights = weights.astype(jnp.bfloat16)
    attended = jnp.einsum('bhlm,bmhd->blhd', weights.astype(jnp.float32), values.astype(jnp.float32)).reshape(samples_here * seq_span, model_width)
    mixed = (layer_norm(attended) * gate_part).astype(jnp.bfloat16)
    output = jnp.dot(mixed, w_out, preferred_element_type=jnp.float32) + embedded.reshape(-1, model_width).astype(jnp.float32)
    return (output, mixed)

def reference(table, history_shard, history_row, lengths, w_in, w_out, cotangent):
    all_rows = (history_shard[:, :, 0] * V_DEV + history_row).astype(jnp.int32)
    group_count = SAMPLES // B_DEV
    grouped_rows = all_rows.reshape(group_count, B_DEV, LMAX)
    grouped_lengths = lengths.reshape(group_count, B_DEV)
    grouped_cot = cotangent.reshape(group_count, B_DEV, LMAX, E)

    def group_step(carry, group):
        grad_table, grad_dense = carry
        rows_here, lengths_here, cot_here = group
        embedded = table[rows_here]
        output, pullback, mixed = jax.vjp(lambda rows_in: hstu_layer(rows_in, w_in, w_out, lengths_here), embedded, has_aux=True)
        row_live = jnp.arange(LMAX)[None, :] < lengths_here[:, None]
        grad_seed = jnp.where(row_live[:, :, None], cot_here, jnp.zeros_like(cot_here))
        flat_seed = grad_seed.reshape(-1, E)
        row_grad, = pullback(flat_seed.astype(jnp.float32))
        grad_dense = grad_dense + jnp.dot(mixed.T, flat_seed, preferred_element_type=jnp.float32)
        grad_table = grad_table + jax.ops.segment_sum(row_grad.reshape(-1, E).astype(jnp.float32), rows_here.reshape(-1), num_segments=VOCAB)
        return ((grad_table, grad_dense), None)
    start_carry = (jnp.zeros((VOCAB, E), jnp.float32), jnp.zeros((E, E), jnp.float32))
    (grad_table, grad_dense), unused = lax.scan(group_step, start_carry, (grouped_rows, grouped_lengths, grouped_cot))
    dense_grad = (grad_dense * (1.0 / math.sqrt(SAMPLES * LMAX))).astype(jnp.bfloat16)
    return (grad_table, dense_grad)
```

```python
import math

import jax
import jax.numpy as jnp
from jax import lax
from jax.sharding import PartitionSpec as P

HEADS = 4


def layer_norm(values):
    average = jnp.mean(values, axis=-1, keepdims=True)
    centred = values - average
    variance = jnp.mean(centred * centred, axis=-1, keepdims=True)
    return centred * lax.rsqrt(variance + 1e-06)


def hstu_layer(embedded, w_in, w_out, lengths):
    samples_here, seq_span, model_width = embedded.shape
    head_dim = model_width // HEADS
    normed = layer_norm(embedded.astype(jnp.float32)).astype(jnp.bfloat16)
    projected = jax.nn.silu(
        jnp.dot(
            normed.reshape(samples_here * seq_span, model_width),
            w_in,
            preferred_element_type=jnp.float32,
        )
    )
    gate_part = projected[:, :model_width]
    shaped = (samples_here, seq_span, HEADS, head_dim)
    values = projected[:, model_width : 2 * model_width].astype(jnp.bfloat16).reshape(shaped)
    queries = projected[:, 2 * model_width : 3 * model_width].astype(jnp.bfloat16).reshape(shaped)
    keys = projected[:, 3 * model_width :].astype(jnp.bfloat16).reshape(shaped)
    scores = jnp.einsum(
        "blhd,bmhd->bhlm", queries.astype(jnp.float32), keys.astype(jnp.float32)
    ) * head_dim ** (-0.5)
    positions = jnp.arange(seq_span)
    live_keys = (positions[None, None, :] <= positions[None, :, None]) & (
        positions[None, None, :] < lengths[:, None, None]
    )
    weights = (
        jnp.where(live_keys[:, None], jax.nn.silu(scores), 0.0)
        / lengths.astype(jnp.float32)[:, None, None, None]
    )
    weights = weights.astype(jnp.bfloat16)
    attended = jnp.einsum(
        "bhlm,bmhd->blhd", weights.astype(jnp.float32), values.astype(jnp.float32)
    ).reshape(samples_here * seq_span, model_width)
    mixed = (layer_norm(attended) * gate_part).astype(jnp.bfloat16)
    output = jnp.dot(mixed, w_out, preferred_element_type=jnp.float32) + embedded.reshape(
        -1, model_width
    ).astype(jnp.float32)
    return (output, mixed)


def pick_rows(index, length):
    return (index[:, None] == jnp.arange(length, dtype=jnp.int32)[None, :]).astype(jnp.bfloat16)


def per_device(table, history_shard, history_row, lengths, w_in, w_out, cotangent):
    shard_rows, model_width = table.shape
    samples_here, seq_span = history_row.shape
    groups = lax.axis_size("table")
    copies = lax.axis_size("dp")
    slot_count = samples_here * seq_span
    capacity = 2 * slot_count // groups
    owners = history_shard[:, :, 0].reshape(-1)
    local_rows = history_row.reshape(-1)
    owner_hits = (owners[:, None] == jnp.arange(groups)[None, :]).astype(jnp.int32)
    slot_rank = jnp.sum((jnp.cumsum(owner_hits, axis=0) - owner_hits) * owner_hits, axis=1)
    position = owners * capacity + slot_rank
    slot_hits = position[:, None] == jnp.arange(groups * capacity, dtype=jnp.int32)[None, :]
    requested = jnp.sum(jnp.where(slot_hits, local_rows[:, None], 0), axis=0).reshape(
        groups, capacity
    )
    incoming = lax.all_to_all(requested, "table", split_axis=0, concat_axis=0, tiled=True).reshape(
        -1
    )
    reply = jnp.dot(
        pick_rows(incoming, shard_rows), table, preferred_element_type=jnp.float32
    ).astype(jnp.bfloat16)
    received = lax.all_to_all(
        reply.reshape(groups, capacity, model_width), "table", split_axis=0, concat_axis=0, tiled=True
    ).reshape(groups * capacity, model_width)
    place = slot_hits.astype(jnp.bfloat16)
    embedded = jnp.dot(place, received, preferred_element_type=jnp.float32).astype(jnp.bfloat16)
    embedded = embedded.reshape(samples_here, seq_span, model_width)
    output, pullback, mixed = jax.vjp(
        lambda rows_in: hstu_layer(rows_in, w_in, w_out, lengths), embedded, has_aux=True
    )
    row_live = jnp.arange(seq_span)[None, :] < lengths[:, None]
    grad_seed = jnp.where(row_live[:, :, None], cotangent, jnp.zeros_like(cotangent))
    flat_seed = grad_seed.reshape(-1, model_width)

    total_slots = slot_count * copies * groups
    grad_scale = 1.0 / math.sqrt(total_slots)
    dense_part = lax.dot_general(
        mixed, flat_seed, (((0,), (0,)), ((), ())), preferred_element_type=jnp.float32
    ).astype(jnp.bfloat16)
    dense_rows = model_width // groups
    dense_terms = lax.all_to_all(
        dense_part.reshape(groups, dense_rows, model_width),
        "table",
        split_axis=0,
        concat_axis=0,
        tiled=True,
    )
    dense_block = jnp.sum(dense_terms.astype(jnp.float32), axis=0).astype(jnp.bfloat16)
    dense_blocks = lax.all_gather(dense_block, "dp", axis=0, tiled=False)
    dense_sum = jnp.sum(dense_blocks.astype(jnp.float32), axis=0) * grad_scale
    dense_grad = lax.all_gather(dense_sum.astype(jnp.bfloat16), "table", axis=0, tiled=True)

    (row_grad,) = pullback(flat_seed.astype(jnp.float32))
    outgoing = lax.dot_general(
        place,
        row_grad.reshape(-1, model_width),
        (((0,), (0,)), ((), ())),
        preferred_element_type=jnp.float32,
    ).astype(jnp.bfloat16)
    arrived = lax.all_to_all(
        outgoing.reshape(groups, capacity, model_width),
        "table",
        split_axis=0,
        concat_axis=0,
        tiled=True,
    ).reshape(groups * capacity, model_width)
    local_grad = lax.dot_general(
        pick_rows(incoming, shard_rows),
        arrived,
        (((0,), (0,)), ((), ())),
        preferred_element_type=jnp.float32,
    ).astype(jnp.bfloat16)
    part_rows = shard_rows // copies
    terms = lax.all_to_all(
        local_grad.reshape(copies, part_rows, model_width),
        "dp",
        split_axis=0,
        concat_axis=0,
        tiled=True,
    )
    summed = jnp.sum(terms.astype(jnp.float32), axis=0).astype(jnp.bfloat16)
    table_grad = lax.all_gather(summed, "dp", axis=0, tiled=True).astype(jnp.float32)
    return (table_grad, dense_grad)


def solution(mesh):
    in_specs = (
        P("table", None),
        P(("dp", "table"), None, None),
        P(("dp", "table"), None),
        P(("dp", "table")),
        P(),
        P(),
        P(("dp", "table"), None, None),
    )
    out_specs = (P("table", None), P())
    return jax.shard_map(
        per_device, mesh=mesh, in_specs=in_specs, out_specs=out_specs, check_vma=False
    )
```

```python
import functools
import math

import jax
import jax.numpy as jnp
from jax import lax
from jax.experimental import pallas as pl
from jax.experimental.pallas import tpu as pltpu
from jax.sharding import PartitionSpec as P

HEADS = 4
NX = 4
NY = 8
MESH = pl.DeviceIdType.MESH


def layer_norm(values):
    average = jnp.mean(values, axis=-1, keepdims=True)
    centred = values - average
    variance = jnp.mean(centred * centred, axis=-1, keepdims=True)
    return centred * lax.rsqrt(variance + 1e-06)


def hstu_layer(embedded, w_in, w_out, lengths):
    samples_here, seq_span, model_width = embedded.shape
    head_dim = model_width // HEADS
    normed = layer_norm(embedded.astype(jnp.float32)).astype(jnp.bfloat16)
    projected = jax.nn.silu(
        jnp.dot(
            normed.reshape(samples_here * seq_span, model_width),
            w_in,
            preferred_element_type=jnp.float32,
        )
    )
    gate_part = projected[:, :model_width]
    shaped = (samples_here, seq_span, HEADS, head_dim)
    values = projected[:, model_width : 2 * model_width].astype(jnp.bfloat16).reshape(shaped)
    queries = projected[:, 2 * model_width : 3 * model_width].astype(jnp.bfloat16).reshape(shaped)
    keys = projected[:, 3 * model_width :].astype(jnp.bfloat16).reshape(shaped)
    scores = jnp.einsum(
        "blhd,bmhd->bhlm", queries.astype(jnp.float32), keys.astype(jnp.float32)
    ) * head_dim ** (-0.5)
    positions = jnp.arange(seq_span)
    live_keys = (positions[None, None, :] <= positions[None, :, None]) & (
        positions[None, None, :] < lengths[:, None, None]
    )
    weights = (
        jnp.where(live_keys[:, None], jax.nn.silu(scores), 0.0)
        / lengths.astype(jnp.float32)[:, None, None, None]
    )
    weights = weights.astype(jnp.bfloat16)
    attended = jnp.einsum(
        "bhlm,bmhd->blhd", weights.astype(jnp.float32), values.astype(jnp.float32)
    ).reshape(samples_here * seq_span, model_width)
    mixed = (layer_norm(attended) * gate_part).astype(jnp.bfloat16)
    output = jnp.dot(mixed, w_out, preferred_element_type=jnp.float32) + embedded.reshape(
        -1, model_width
    ).astype(jnp.float32)
    return (output, mixed)


def pick_rows(index, length):
    return (index[:, None] == jnp.arange(length, dtype=jnp.int32)[None, :]).astype(jnp.bfloat16)


def send(src, dst, send_sem, recv_sem, **where):
    return pltpu.make_async_remote_copy(
        src_ref=src,
        dst_ref=dst,
        send_sem=send_sem,
        recv_sem=recv_sem,
        device_id=where,
        device_id_type=MESH,
    )


def each(start, stop, body):
    def step(i, carry):
        body(i)
        return carry

    lax.fori_loop(start, stop, step, 0)


def exchange_kernel(
    scale,
    outgoing,
    dense_part,
    incoming,
    table_out,
    dense_out,
    arrived,
    dense_arr,
    part,
    x_in,
    x_sum,
    y_in,
    whole,
    dx_out,
    dx_in,
    dy_in,
    d_row,
    d_all,
    z_s,
    z_r,
    dz_s,
    dz_r,
    x_s,
    x_r,
    y_s,
    y_r,
    gy_s,
    gy_r,
    gx_s,
    gx_r,
    dx_s,
    dx_r,
    dy_s,
    dy_r,
    dgx_s,
    dgx_r,
    dgz_s,
    dgz_r,
):
    nz, cap, width = outgoing.shape
    rows = table_out.shape[0]
    x_rows = rows // NX
    half = x_rows // 2
    me = lax.axis_index("table")
    spot = lax.axis_index("dp")
    x = spot // NY
    y = lax.rem(spot, NY)
    f32, bf16 = jnp.float32, jnp.bfloat16

    def zp(k):
        return lax.rem(me + k, nz)

    def xp(k):
        return lax.rem(x + k, NX)

    def yp(k):
        return lax.rem(y + k, NY)

    def at_x(px):
        return px * NY + y

    def at_y(py):
        return x * NY + py

    barrier = pltpu.get_barrier_semaphore()

    def greet(axis, peer):
        pl.semaphore_signal(barrier, inc=1, device_id={axis: peer}, device_id_type=MESH)

    each(1, nz, lambda k: greet("table", zp(k)))
    each(1, NX, lambda k: greet("dp", at_x(xp(k))))
    each(1, NY, lambda k: greet("dp", at_y(yp(k))))
    pl.semaphore_wait(barrier, nz - 1 + NX - 1 + NY - 1)

    def z_copy(p):
        return send(outgoing.at[p], arrived.at[me], z_s.at[p], z_r.at[me], table=p)

    def z_wait(p):
        send(outgoing.at[p], arrived.at[p], z_s.at[p], z_r.at[p], table=p).wait_recv()

    def dz_copy(p):
        return send(dense_part.at[p], dense_arr.at[me], dz_s.at[p], dz_r.at[me], table=p)

    def dz_wait(p):
        send(dense_part.at[p], dense_arr.at[p], dz_s.at[p], dz_r.at[p], table=p).wait_recv()

    each(1, nz, lambda k: z_copy(zp(k)).start())
    each(1, nz, lambda k: dz_copy(zp(k)).start())
    arrived[me] = outgoing[me]
    dense_arr[me] = dense_part[me]
    each(1, nz, lambda k: z_wait(zp(k)))

    def x_copy(p, c):
        return send(part.at[p, c], x_in.at[x, c], x_s.at[p, c], x_r.at[x, c], dp=at_x(p))

    def x_wait(p, c):
        send(part.at[p, c], x_in.at[p, c], x_s.at[p, c], x_r.at[p, c], dp=at_x(p)).wait_recv()

    def make_part(p):
        line = lax.broadcasted_iota(jnp.int32, (x_rows, nz * cap), 0) + p * x_rows
        pick = (line == incoming[...]).astype(f32).astype(bf16)
        got = arrived[...].reshape(nz * cap, width)
        block = jnp.dot(pick, got, preferred_element_type=f32).astype(bf16)
        for c in range(NY):
            part[p, c] = block[
                (c % 2) * half : (c % 2 + 1) * half, (c // 2) * 128 : (c // 2 + 1) * 128
            ]

    def x_stage(k):
        p = xp(k)
        make_part(p)
        each(1, NY + 1, lambda j: x_copy(p, yp(j)).start())

    each(1, NX, x_stage)
    make_part(x)

    def y_copy(c):
        return send(x_sum.at[c], y_in.at[y], y_s.at[c], y_r.at[y], dp=at_y(c))

    def y_wait(c):
        send(x_sum.at[c], y_in.at[c], y_s.at[c], y_r.at[c], dp=at_y(c)).wait_recv()

    def sum_x(c):
        total = part[x, c].astype(f32)
        for k in range(1, NX):
            p = xp(k)
            x_wait(p, c)
            total = total + x_in[p, c].astype(f32)
        x_sum[c] = total.astype(bf16)

    def y_stage(j):
        c = yp(j)
        sum_x(c)
        y_copy(c).start()

    each(1, NY, y_stage)
    sum_x(y)

    def dx_copy(p):
        return send(dx_out.at[p], dx_in.at[x], dx_s.at[p], dx_r.at[x], dp=at_x(p))

    def dx_wait(p):
        send(dx_out.at[p], dx_in.at[p], dx_s.at[p], dx_r.at[p], dp=at_x(p)).wait_recv()

    each(1, nz, lambda k: dz_wait(zp(k)))
    dense_sum = dense_arr[0].astype(f32)
    for k in range(1, nz):
        dense_sum = dense_sum + dense_arr[k].astype(f32)
    dense_sum = dense_sum.astype(bf16)
    for c in range(NX):
        dx_out[c] = dense_sum[:, c * 128 : (c + 1) * 128]
    each(1, NX, lambda k: dx_copy(xp(k)).start())

    total = x_sum[y].astype(f32)
    for j in range(1, NY):
        c = yp(j)
        y_wait(c)
        total = total + y_in[c].astype(f32)
    whole[x, y] = total.astype(bf16)

    def gy_copy(p):
        return send(whole.at[x, y], whole.at[x, y], gy_s.at[p], gy_r.at[y], dp=at_y(p))

    def gy_wait(p):
        send(whole.at[x, p], whole.at[x, p], gy_s.at[p], gy_r.at[p], dp=at_y(p)).wait_recv()

    def gx_copy(p, c):
        return send(whole.at[x, c], whole.at[x, c], gx_s.at[p, c], gx_r.at[x, c], dp=at_x(p))

    def gx_wait(p, c):
        send(whole.at[p, c], whole.at[p, c], gx_s.at[p, c], gx_r.at[p, c], dp=at_x(p)).wait_recv()

    each(1, NY, lambda k: gy_copy(yp(k)).start())
    each(1, NX, lambda k: gx_copy(xp(k), y).start())

    def dy_copy(p):
        return send(dy_in.at[y], dy_in.at[y], dy_s.at[p], dy_r.at[y], dp=at_y(p))

    def dy_wait(p):
        send(dy_in.at[p], dy_in.at[p], dy_s.at[p], dy_r.at[p], dp=at_y(p)).wait_recv()

    dx_in[x] = dx_out[x]
    each(1, NX, lambda k: dx_wait(xp(k)))
    d_total = dx_in[0].astype(f32)
    for k in range(1, NX):
        d_total = d_total + dx_in[k].astype(f32)
    dy_in[y] = d_total.astype(bf16)
    each(1, NY, lambda k: dy_copy(yp(k)).start())

    def pass_on(j):
        c = yp(j)
        gy_wait(c)
        each(1, NX, lambda k: gx_copy(xp(k), c).start())

    each(1, NY // 2, pass_on)

    def dgx_copy(p):
        return send(d_row.at[x], d_row.at[x], dgx_s.at[p], dgx_r.at[x], dp=at_x(p))

    def dgx_wait(p):
        send(d_row.at[p], d_row.at[p], dgx_s.at[p], dgx_r.at[p], dp=at_x(p)).wait_recv()

    each(1, NY, lambda k: dy_wait(yp(k)))
    d_total = dy_in[0].astype(f32)
    for k in range(1, NY):
        d_total = d_total + dy_in[k].astype(f32)
    d_row[x] = (d_total * scale).astype(bf16)
    each(1, NX, lambda k: dgx_copy(xp(k)).start())
    each(NY // 2, NY, pass_on)

    def dgz_copy(p):
        return send(d_row, d_all.at[me], dgz_s.at[p], dgz_r.at[me], table=p)

    def dgz_wait(p):
        send(d_row, d_all.at[p], dgz_s.at[p], dgz_r.at[p], table=p).wait_recv()

    each(1, NX, lambda k: dgx_wait(xp(k)))
    each(1, nz, lambda k: dgz_copy(zp(k)).start())
    d_all[me] = d_row[...]

    def gx_wait_all(k):
        each(0, NY, lambda c: gx_wait(xp(k), c))

    each(1, NX, gx_wait_all)
    for px in range(NX):
        for c in range(NY):
            table_out[
                px * x_rows + (c % 2) * half : px * x_rows + (c % 2 + 1) * half,
                (c // 2) * 128 : (c // 2 + 1) * 128,
            ] = whole[px, c]
    each(1, nz, lambda k: dgz_wait(zp(k)))
    for t in range(nz):
        for c in range(NX):
            dense_out[t * cap : (t + 1) * cap, c * 128 : (c + 1) * 128] = d_all[t, c]

    def sent_z(k):
        p = zp(k)
        z_copy(p).wait_send()
        dz_copy(p).wait_send()
        dgz_copy(p).wait_send()

    def sent_x(k):
        p = xp(k)
        dx_copy(p).wait_send()
        dgx_copy(p).wait_send()

        def pieces(c):
            x_copy(p, c).wait_send()
            gx_copy(p, c).wait_send()

        each(0, NY, pieces)

    def sent_y(k):
        p = yp(k)
        y_copy(p).wait_send()
        gy_copy(p).wait_send()
        dy_copy(p).wait_send()

    each(1, nz, sent_z)
    each(1, NX, sent_x)
    each(1, NY, sent_y)


def exchange(outgoing, dense_part, incoming, shard_rows, scale):
    groups, capacity, width = outgoing.shape
    bf16 = jnp.bfloat16
    piece = (shard_rows // NX // 2, 128)
    small = (capacity, 128)
    vmem = pl.BlockSpec(memory_space=pltpu.VMEM)
    dma = pltpu.SemaphoreType.DMA

    def pair(*dims):
        return [dma(dims), dma(dims)]

    return pl.pallas_call(
        functools.partial(exchange_kernel, scale),
        out_shape=(
            jax.ShapeDtypeStruct((shard_rows, width), bf16),
            jax.ShapeDtypeStruct((groups * capacity, width), bf16),
        ),
        in_specs=[vmem] * 3,
        out_specs=(vmem, vmem),
        scratch_shapes=[
            pltpu.VMEM((groups, capacity, width), bf16),
            pltpu.VMEM((groups, capacity, width), bf16),
            pltpu.VMEM((NX, NY) + piece, bf16),
            pltpu.VMEM((NX, NY) + piece, bf16),
            pltpu.VMEM((NY,) + piece, bf16),
            pltpu.VMEM((NY,) + piece, bf16),
            pltpu.VMEM((NX, NY) + piece, bf16),
            pltpu.VMEM((NX,) + small, bf16),
            pltpu.VMEM((NX,) + small, bf16),
            pltpu.VMEM((NY,) + small, bf16),
            pltpu.VMEM((NX,) + small, bf16),
            pltpu.VMEM((groups, NX) + small, bf16),
        ]
        + pair(groups)
        + pair(groups)
        + pair(NX, NY)
        + pair(NY)
        + pair(NY)
        + pair(NX, NY)
        + pair(NX)
        + pair(NY)
        + pair(NX)
        + pair(groups),
        compiler_params=pltpu.CompilerParams(
            collective_id=0, has_side_effects=True, vmem_limit_bytes=32 << 20
        ),
    )(outgoing, dense_part, incoming)


def per_device(table, history_shard, history_row, lengths, w_in, w_out, cotangent):
    shard_rows, model_width = table.shape
    samples_here, seq_span = history_row.shape
    groups = lax.axis_size("table")
    copies = lax.axis_size("dp")
    slot_count = samples_here * seq_span
    capacity = 2 * slot_count // groups
    owners = history_shard[:, :, 0].reshape(-1)
    local_rows = history_row.reshape(-1)
    owner_hits = (owners[:, None] == jnp.arange(groups)[None, :]).astype(jnp.int32)
    slot_rank = jnp.sum((jnp.cumsum(owner_hits, axis=0) - owner_hits) * owner_hits, axis=1)
    position = owners * capacity + slot_rank
    slot_hits = position[:, None] == jnp.arange(groups * capacity, dtype=jnp.int32)[None, :]
    requested = jnp.sum(jnp.where(slot_hits, local_rows[:, None], 0), axis=0).reshape(
        groups, capacity
    )
    incoming = lax.all_to_all(requested, "table", split_axis=0, concat_axis=0, tiled=True).reshape(
        -1
    )
    reply = jnp.dot(
        pick_rows(incoming, shard_rows), table, preferred_element_type=jnp.float32
    ).astype(jnp.bfloat16)
    received = lax.all_to_all(
        reply.reshape(groups, capacity, model_width), "table", split_axis=0, concat_axis=0, tiled=True
    ).reshape(groups * capacity, model_width)
    place = slot_hits.astype(jnp.bfloat16)
    embedded = jnp.dot(place, received, preferred_element_type=jnp.float32).astype(jnp.bfloat16)
    embedded = embedded.reshape(samples_here, seq_span, model_width)
    output, pullback, mixed = jax.vjp(
        lambda rows_in: hstu_layer(rows_in, w_in, w_out, lengths), embedded, has_aux=True
    )
    row_live = jnp.arange(seq_span)[None, :] < lengths[:, None]
    grad_seed = jnp.where(row_live[:, :, None], cotangent, jnp.zeros_like(cotangent))
    flat_seed = grad_seed.reshape(-1, model_width)

    total_slots = slot_count * copies * groups
    grad_scale = 1.0 / math.sqrt(total_slots)
    dense_part = lax.dot_general(
        mixed, flat_seed, (((0,), (0,)), ((), ())), preferred_element_type=jnp.float32
    ).astype(jnp.bfloat16)
    (row_grad,) = pullback(flat_seed.astype(jnp.float32))
    outgoing = lax.dot_general(
        place,
        row_grad.reshape(-1, model_width),
        (((0,), (0,)), ((), ())),
        preferred_element_type=jnp.float32,
    ).astype(jnp.bfloat16)
    table_sum, dense_grad = exchange(
        outgoing.reshape(groups, capacity, model_width),
        dense_part.reshape(groups, capacity, model_width),
        incoming.reshape(1, groups * capacity),
        shard_rows,
        grad_scale,
    )
    table_grad = table_sum.astype(jnp.float32)
    return (table_grad, dense_grad)


def solution(mesh):
    in_specs = (
        P("table", None),
        P(("dp", "table"), None, None),
        P(("dp", "table"), None),
        P(("dp", "table")),
        P(),
        P(),
        P(("dp", "table"), None, None),
    )
    out_specs = (P("table", None), P())
    return jax.shard_map(
        per_device, mesh=mesh, in_specs=in_specs, out_specs=out_specs, check_vma=False
    )
```

```python
import functools
import math

import jax
import jax.numpy as jnp
from jax import lax
from jax.experimental import pallas as pl
from jax.experimental.pallas import tpu as pltpu
from jax.sharding import PartitionSpec as P

HEADS = 4
NX = 4
NY = 8
MESH = pl.DeviceIdType.MESH


def layer_norm(values):
    average = jnp.mean(values, axis=-1, keepdims=True)
    centred = values - average
    variance = jnp.mean(centred * centred, axis=-1, keepdims=True)
    return centred * lax.rsqrt(variance + 1e-06)


def hstu_layer(embedded, w_in, w_out, lengths):
    samples_here, seq_span, model_width = embedded.shape
    head_dim = model_width // HEADS
    normed = layer_norm(embedded.astype(jnp.float32)).astype(jnp.bfloat16)
    projected = jax.nn.silu(
        jnp.dot(
            normed.reshape(samples_here * seq_span, model_width),
            w_in,
            preferred_element_type=jnp.float32,
        )
    )
    gate_part = projected[:, :model_width]
    shaped = (samples_here, seq_span, HEADS, head_dim)
    values = projected[:, model_width : 2 * model_width].astype(jnp.bfloat16).reshape(shaped)
    queries = projected[:, 2 * model_width : 3 * model_width].astype(jnp.bfloat16).reshape(shaped)
    keys = projected[:, 3 * model_width :].astype(jnp.bfloat16).reshape(shaped)
    scores = jnp.einsum(
        "blhd,bmhd->bhlm", queries.astype(jnp.float32), keys.astype(jnp.float32)
    ) * head_dim ** (-0.5)
    positions = jnp.arange(seq_span)
    live_keys = (positions[None, None, :] <= positions[None, :, None]) & (
        positions[None, None, :] < lengths[:, None, None]
    )
    weights = (
        jnp.where(live_keys[:, None], jax.nn.silu(scores), 0.0)
        / lengths.astype(jnp.float32)[:, None, None, None]
    )
    weights = weights.astype(jnp.bfloat16)
    attended = jnp.einsum(
        "bhlm,bmhd->blhd", weights.astype(jnp.float32), values.astype(jnp.float32)
    ).reshape(samples_here * seq_span, model_width)
    mixed = (layer_norm(attended) * gate_part).astype(jnp.bfloat16)
    output = jnp.dot(mixed, w_out, preferred_element_type=jnp.float32) + embedded.reshape(
        -1, model_width
    ).astype(jnp.float32)
    return (output, mixed)


def send(src, dst, send_sem, recv_sem, **where):
    return pltpu.make_async_remote_copy(
        src_ref=src,
        dst_ref=dst,
        send_sem=send_sem,
        recv_sem=recv_sem,
        device_id=where,
        device_id_type=MESH,
    )


def each(start, stop, body):
    def step(i, carry):
        body(i)
        return carry

    lax.fori_loop(start, stop, step, 0)


def exchange_kernel(
    scale,
    outgoing,
    dense_part,
    incoming,
    table_out,
    dense_out,
    arrived,
    dense_arr,
    part,
    x_in,
    x_sum,
    y_in,
    whole,
    dx_out,
    dx_in,
    dy_in,
    d_row,
    d_all,
    z_s,
    z_r,
    dz_s,
    dz_r,
    x_s,
    x_r,
    y_s,
    y_r,
    gy_s,
    gy_r,
    gx_s,
    gx_r,
    dx_s,
    dx_r,
    dy_s,
    dy_r,
    dgx_s,
    dgx_r,
    dgz_s,
    dgz_r,
):
    nz, cap, width = outgoing.shape
    rows = table_out.shape[0]
    x_rows = rows // NX
    half = x_rows // 2
    me = lax.axis_index("table")
    spot = lax.axis_index("dp")
    x = spot // NY
    y = lax.rem(spot, NY)
    f32, bf16 = jnp.float32, jnp.bfloat16

    def zp(k):
        return lax.rem(me + k, nz)

    def xp(k):
        return lax.rem(x + k, NX)

    def yp(k):
        return lax.rem(y + k, NY)

    def at_x(px):
        return px * NY + y

    def at_y(py):
        return x * NY + py

    barrier = pltpu.get_barrier_semaphore()

    def greet(axis, peer):
        pl.semaphore_signal(barrier, inc=1, device_id={axis: peer}, device_id_type=MESH)

    each(1, nz, lambda k: greet("table", zp(k)))
    each(1, NX, lambda k: greet("dp", at_x(xp(k))))
    each(1, NY, lambda k: greet("dp", at_y(yp(k))))
    pl.semaphore_wait(barrier, nz - 1 + NX - 1 + NY - 1)

    def z_copy(p):
        return send(outgoing.at[p], arrived.at[me], z_s.at[p], z_r.at[me], table=p)

    def z_wait(p):
        send(outgoing.at[p], arrived.at[p], z_s.at[p], z_r.at[p], table=p).wait_recv()

    def dz_copy(p):
        return send(dense_part.at[p], dense_arr.at[me], dz_s.at[p], dz_r.at[me], table=p)

    def dz_wait(p):
        send(dense_part.at[p], dense_arr.at[p], dz_s.at[p], dz_r.at[p], table=p).wait_recv()

    each(1, nz, lambda k: z_copy(zp(k)).start())
    arrived[me] = outgoing[me]
    dense_arr[me] = dense_part[me]
    each(1, nz, lambda k: z_wait(zp(k)))
    each(1, nz, lambda k: dz_copy(zp(k)).start())

    def x_copy(p, c):
        return send(part.at[p, c], x_in.at[x, c], x_s.at[p, c], x_r.at[x, c], dp=at_x(p))

    def x_wait(p, c):
        send(part.at[p, c], x_in.at[p, c], x_s.at[p, c], x_r.at[p, c], dp=at_x(p)).wait_recv()

    def make_part(p):
        line = lax.broadcasted_iota(jnp.int32, (x_rows, nz * cap), 0) + p * x_rows
        pick = (line == incoming[...]).astype(f32).astype(bf16)
        got = arrived[...].reshape(nz * cap, width)
        block = jnp.dot(pick, got, preferred_element_type=f32).astype(bf16)
        for c in range(NY):
            part[p, c] = block[
                (c % 2) * half : (c % 2 + 1) * half, (c // 2) * 128 : (c // 2 + 1) * 128
            ]

    def x_stage(k):
        p = xp(k)
        make_part(p)
        each(1, NY + 1, lambda j: x_copy(p, yp(j)).start())

    each(1, NX, x_stage)
    make_part(x)

    def y_copy(c):
        return send(x_sum.at[c], y_in.at[y], y_s.at[c], y_r.at[y], dp=at_y(c))

    def y_wait(c):
        send(x_sum.at[c], y_in.at[c], y_s.at[c], y_r.at[c], dp=at_y(c)).wait_recv()

    def sum_x(c):
        total = part[x, c].astype(f32)
        for k in range(1, NX):
            p = xp(k)
            x_wait(p, c)
            total = total + x_in[p, c].astype(f32)
        x_sum[c] = total.astype(bf16)

    def y_stage(j):
        c = yp(j)
        sum_x(c)
        y_copy(c).start()

    each(1, NY, y_stage)
    sum_x(y)

    def dx_copy(p):
        return send(dx_out.at[p], dx_in.at[x], dx_s.at[p], dx_r.at[x], dp=at_x(p))

    def dx_wait(p):
        send(dx_out.at[p], dx_in.at[p], dx_s.at[p], dx_r.at[p], dp=at_x(p)).wait_recv()

    each(1, nz, lambda k: dz_wait(zp(k)))
    dense_sum = dense_arr[0].astype(f32)
    for k in range(1, nz):
        dense_sum = dense_sum + dense_arr[k].astype(f32)
    dense_sum = dense_sum.astype(bf16)
    for c in range(NX):
        dx_out[c] = dense_sum[:, c * 128 : (c + 1) * 128]
    each(1, NX, lambda k: dx_copy(xp(k)).start())

    total = x_sum[y].astype(f32)
    for j in range(1, NY):
        c = yp(j)
        y_wait(c)
        total = total + y_in[c].astype(f32)
    whole[x, y] = total.astype(bf16)

    def gy_copy(p):
        return send(whole.at[x, y], whole.at[x, y], gy_s.at[p], gy_r.at[y], dp=at_y(p))

    def gy_wait(p):
        send(whole.at[x, p], whole.at[x, p], gy_s.at[p], gy_r.at[p], dp=at_y(p)).wait_recv()

    def gx_copy(p, c):
        return send(whole.at[x, c], whole.at[x, c], gx_s.at[p, c], gx_r.at[x, c], dp=at_x(p))

    def gx_wait(p, c):
        send(whole.at[p, c], whole.at[p, c], gx_s.at[p, c], gx_r.at[p, c], dp=at_x(p)).wait_recv()

    each(1, NY, lambda k: gy_copy(yp(k)).start())
    each(1, NX, lambda k: gx_copy(xp(k), y).start())

    def dy_copy(p):
        return send(dy_in.at[y], dy_in.at[y], dy_s.at[p], dy_r.at[y], dp=at_y(p))

    def dy_wait(p):
        send(dy_in.at[p], dy_in.at[p], dy_s.at[p], dy_r.at[p], dp=at_y(p)).wait_recv()

    dx_in[x] = dx_out[x]
    each(1, NX, lambda k: dx_wait(xp(k)))
    d_total = dx_in[0].astype(f32)
    for k in range(1, NX):
        d_total = d_total + dx_in[k].astype(f32)
    dy_in[y] = d_total.astype(bf16)
    each(1, NY, lambda k: dy_copy(yp(k)).start())

    def pass_on(j):
        c = yp(j)
        gy_wait(c)
        each(1, NX, lambda k: gx_copy(xp(k), c).start())

    each(1, NY // 2, pass_on)

    def dgx_copy(p):
        return send(d_row.at[x], d_row.at[x], dgx_s.at[p], dgx_r.at[x], dp=at_x(p))

    def dgx_wait(p):
        send(d_row.at[p], d_row.at[p], dgx_s.at[p], dgx_r.at[p], dp=at_x(p)).wait_recv()

    each(1, NY, lambda k: dy_wait(yp(k)))
    d_total = dy_in[0].astype(f32)
    for k in range(1, NY):
        d_total = d_total + dy_in[k].astype(f32)
    d_row[x] = (d_total * scale).astype(bf16)
    each(1, NX, lambda k: dgx_copy(xp(k)).start())
    each(NY // 2, NY, pass_on)

    def dgz_copy(p):
        return send(d_row, d_all.at[me], dgz_s.at[p], dgz_r.at[me], table=p)

    def dgz_wait(p):
        send(d_row, d_all.at[p], dgz_s.at[p], dgz_r.at[p], table=p).wait_recv()

    each(1, NX, lambda k: dgx_wait(xp(k)))
    each(1, nz, lambda k: dgz_copy(zp(k)).start())
    d_all[me] = d_row[...]

    def gx_wait_all(k):
        each(0, NY, lambda c: gx_wait(xp(k), c))

    each(1, NX, gx_wait_all)
    for px in range(NX):
        for c in range(NY):
            table_out[
                px * x_rows + (c % 2) * half : px * x_rows + (c % 2 + 1) * half,
                (c // 2) * 128 : (c // 2 + 1) * 128,
            ] = whole[px, c]
    each(1, nz, lambda k: dgz_wait(zp(k)))
    for t in range(nz):
        for c in range(NX):
            dense_out[t * cap : (t + 1) * cap, c * 128 : (c + 1) * 128] = d_all[t, c]

    def sent_z(k):
        p = zp(k)
        z_copy(p).wait_send()
        dz_copy(p).wait_send()
        dgz_copy(p).wait_send()

    def sent_x(k):
        p = xp(k)
        dx_copy(p).wait_send()
        dgx_copy(p).wait_send()

        def pieces(c):
            x_copy(p, c).wait_send()
            gx_copy(p, c).wait_send()

        each(0, NY, pieces)

    def sent_y(k):
        p = yp(k)
        y_copy(p).wait_send()
        gy_copy(p).wait_send()
        dy_copy(p).wait_send()

    each(1, nz, sent_z)
    each(1, NX, sent_x)
    each(1, NY, sent_y)


def exchange(outgoing, dense_part, incoming, shard_rows, scale):
    groups, capacity, width = outgoing.shape
    bf16 = jnp.bfloat16
    piece = (shard_rows // NX // 2, 128)
    small = (capacity, 128)
    vmem = pl.BlockSpec(memory_space=pltpu.VMEM)
    dma = pltpu.SemaphoreType.DMA

    def pair(*dims):
        return [dma(dims), dma(dims)]

    return pl.pallas_call(
        functools.partial(exchange_kernel, scale),
        out_shape=(
            jax.ShapeDtypeStruct((shard_rows, width), bf16),
            jax.ShapeDtypeStruct((groups * capacity, width), bf16),
        ),
        in_specs=[vmem] * 3,
        out_specs=(vmem, vmem),
        scratch_shapes=[
            pltpu.VMEM((groups, capacity, width), bf16),
            pltpu.VMEM((groups, capacity, width), bf16),
            pltpu.VMEM((NX, NY) + piece, bf16),
            pltpu.VMEM((NX, NY) + piece, bf16),
            pltpu.VMEM((NY,) + piece, bf16),
            pltpu.VMEM((NY,) + piece, bf16),
            pltpu.VMEM((NX, NY) + piece, bf16),
            pltpu.VMEM((NX,) + small, bf16),
            pltpu.VMEM((NX,) + small, bf16),
            pltpu.VMEM((NY,) + small, bf16),
            pltpu.VMEM((NX,) + small, bf16),
            pltpu.VMEM((groups, NX) + small, bf16),
        ]
        + pair(groups)
        + pair(groups)
        + pair(NX, NY)
        + pair(NY)
        + pair(NY)
        + pair(NX, NY)
        + pair(NX)
        + pair(NY)
        + pair(NX)
        + pair(groups),
        compiler_params=pltpu.CompilerParams(
            collective_id=0, has_side_effects=True, vmem_limit_bytes=32 << 20
        ),
    )(outgoing, dense_part, incoming)


def dot_first(a, b):
    return lax.dot_general(a, b, (((0,), (0,)), ((), ())), preferred_element_type=jnp.float32)


def hot(shape, index):
    line = lax.broadcasted_iota(jnp.int32, shape, 0)
    return (line == index).astype(jnp.float32).astype(jnp.bfloat16)


def fetch_kernel(
    table,
    owners,
    rows,
    embedded,
    position,
    incoming,
    req_out,
    req_in,
    reply,
    got,
    q_s,
    q_r,
    r_s,
    r_r,
):
    nz, cap, width = got.shape
    slots = owners.shape[1]
    shard_rows = table.shape[0]
    per = 128 // cap
    me = lax.axis_index("table")
    f32, bf16 = jnp.float32, jnp.bfloat16

    def zp(k):
        return lax.rem(me + k, nz)

    barrier = pltpu.get_barrier_semaphore()
    each(
        1,
        nz,
        lambda k: pl.semaphore_signal(
            barrier, inc=1, device_id={"table": zp(k)}, device_id_type=MESH
        ),
    )
    own = owners[...]
    hits = (lax.broadcasted_iota(jnp.int32, (nz, slots), 0) == own).astype(f32)
    earlier = (
        lax.broadcasted_iota(jnp.int32, (slots, slots), 0)
        < lax.broadcasted_iota(jnp.int32, (slots, slots), 1)
    ).astype(f32)
    ahead = jnp.dot(hits.astype(bf16), earlier.astype(bf16), preferred_element_type=f32)
    rank = jnp.sum(hits * ahead, axis=0, keepdims=True).astype(jnp.int32)
    place = own * cap + rank
    position[...] = place
    pick = hot((nz * 128, slots), own * 128 + lax.rem(me, per) * cap + rank)
    wanted = rows[...]
    high = lax.shift_right_logical(wanted, 8)
    low = wanted & 255
    which = lax.broadcasted_iota(jnp.int32, (8, slots), 0)
    both = jnp.where(which == 0, high, jnp.where(which == 1, low, 0)).astype(f32).astype(bf16)
    found = lax.dot_general(both, pick, (((1,), (1,)), ((), ())), preferred_element_type=f32)
    asked = (found[0:1] * 256.0 + found[1:2]).astype(jnp.int32)
    for p in range(nz):
        req_out[p] = asked[:, p * 128 : (p + 1) * 128]
    pl.semaphore_wait(barrier, nz - 1)

    def q_copy(p):
        return send(req_out.at[p], req_in.at[me], q_s.at[p], q_r.at[me], table=p)

    def q_wait(p):
        send(req_out.at[p], req_in.at[p], q_s.at[p], q_r.at[p], table=p).wait_recv()

    def r_copy(p):
        return send(reply.at[p], got.at[me], r_s.at[p], r_r.at[me], table=p)

    def r_wait(p):
        send(reply.at[p], got.at[p], r_s.at[p], r_r.at[p], table=p).wait_recv()

    each(1, nz, lambda k: q_copy(zp(k)).start())
    req_in[me] = req_out[me]
    each(1, nz, lambda k: q_wait(zp(k)))
    for g in range(nz // per):
        line = req_in[g * per]
        for j in range(1, per):
            line = line + req_in[g * per + j]
        incoming[:, g * 128 : (g + 1) * 128] = line
        block = dot_first(hot((shard_rows, 128), line), table[...]).astype(bf16)
        for j in range(per):
            reply[g * per + j] = block[j * cap : (j + 1) * cap]
    each(1, nz, lambda k: r_copy(zp(k)).start())
    got[me] = reply[me]
    each(1, nz, lambda k: r_wait(zp(k)))
    spread = hot((nz * cap, slots), place)
    embedded[...] = dot_first(spread, got[...].reshape(nz * cap, width)).astype(bf16)

    def sent(k):
        q_copy(zp(k)).wait_send()
        r_copy(zp(k)).wait_send()

    each(1, nz, sent)


def fetch(table, owners, rows, groups, capacity):
    shard_rows, width = table.shape
    slots = owners.shape[1]
    vmem = pl.BlockSpec(memory_space=pltpu.VMEM)
    dma = pltpu.SemaphoreType.DMA
    return pl.pallas_call(
        fetch_kernel,
        out_shape=(
            jax.ShapeDtypeStruct((slots, width), jnp.bfloat16),
            jax.ShapeDtypeStruct((1, slots), jnp.int32),
            jax.ShapeDtypeStruct((1, groups * capacity), jnp.int32),
        ),
        in_specs=[vmem] * 3,
        out_specs=(vmem, vmem, vmem),
        scratch_shapes=[
            pltpu.VMEM((groups, 1, 128), jnp.int32),
            pltpu.VMEM((groups, 1, 128), jnp.int32),
            pltpu.VMEM((groups, capacity, width), jnp.bfloat16),
            pltpu.VMEM((groups, capacity, width), jnp.bfloat16),
            dma((groups,)),
            dma((groups,)),
            dma((groups,)),
            dma((groups,)),
        ],
        compiler_params=pltpu.CompilerParams(
            collective_id=1, has_side_effects=True, vmem_limit_bytes=32 << 20
        ),
    )(table, owners, rows)


def per_device(table, history_shard, history_row, lengths, w_in, w_out, cotangent):
    shard_rows, model_width = table.shape
    samples_here, seq_span = history_row.shape
    groups = lax.axis_size("table")
    copies = lax.axis_size("dp")
    slot_count = samples_here * seq_span
    capacity = 2 * slot_count // groups
    embedded, position, incoming = fetch(
        table,
        history_shard.reshape(1, slot_count),
        history_row.reshape(1, slot_count),
        groups,
        capacity,
    )
    slots_at = jnp.arange(groups * capacity, dtype=jnp.int32)[:, None]
    place = (slots_at == position).astype(jnp.bfloat16)
    embedded = embedded.reshape(samples_here, seq_span, model_width)
    output, pullback, mixed = jax.vjp(
        lambda rows_in: hstu_layer(rows_in, w_in, w_out, lengths), embedded, has_aux=True
    )
    row_live = jnp.arange(seq_span)[None, :] < lengths[:, None]
    grad_seed = jnp.where(row_live[:, :, None], cotangent, jnp.zeros_like(cotangent))
    flat_seed = grad_seed.reshape(-1, model_width)

    total_slots = slot_count * copies * groups
    grad_scale = 1.0 / math.sqrt(total_slots)
    dense_part = lax.dot_general(
        mixed, flat_seed, (((0,), (0,)), ((), ())), preferred_element_type=jnp.float32
    ).astype(jnp.bfloat16)
    (row_grad,) = pullback(flat_seed.astype(jnp.float32))
    outgoing = jnp.dot(
        place, row_grad.reshape(-1, model_width), preferred_element_type=jnp.float32
    ).astype(jnp.bfloat16)
    table_sum, dense_grad = exchange(
        outgoing.reshape(groups, capacity, model_width),
        dense_part.reshape(groups, capacity, model_width),
        incoming,
        shard_rows,
        grad_scale,
    )
    table_grad = table_sum.astype(jnp.float32)
    return (table_grad, dense_grad)


def solution(mesh):
    in_specs = (
        P("table", None),
        P(("dp", "table"), None, None),
        P(("dp", "table"), None),
        P(("dp", "table")),
        P(),
        P(),
        P(("dp", "table"), None, None),
    )
    out_specs = (P("table", None), P())
    return jax.shard_map(
        per_device, mesh=mesh, in_specs=in_specs, out_specs=out_specs, check_vma=False
    )
```

```python
import functools
import math

import jax
import jax.numpy as jnp
from jax import lax
from jax.experimental import pallas as pl
from jax.experimental.pallas import tpu as pltpu
from jax.sharding import PartitionSpec as P

HEADS = 4
NX = 4
NY = 8
MESH = pl.DeviceIdType.MESH


def layer_norm(values):
    average = jnp.mean(values, axis=-1, keepdims=True)
    centred = values - average
    variance = jnp.mean(centred * centred, axis=-1, keepdims=True)
    return centred * lax.rsqrt(variance + 1e-06)


def hstu_layer(embedded, w_in, w_out, lengths):
    samples_here, seq_span, model_width = embedded.shape
    head_dim = model_width // HEADS
    normed = layer_norm(embedded.astype(jnp.float32)).astype(jnp.bfloat16)
    projected = jax.nn.silu(
        jnp.dot(
            normed.reshape(samples_here * seq_span, model_width),
            w_in,
            preferred_element_type=jnp.float32,
        )
    )
    gate_part = projected[:, :model_width]
    shaped = (samples_here, seq_span, HEADS, head_dim)
    values = projected[:, model_width : 2 * model_width].astype(jnp.bfloat16).reshape(shaped)
    queries = projected[:, 2 * model_width : 3 * model_width].astype(jnp.bfloat16).reshape(shaped)
    keys = projected[:, 3 * model_width :].astype(jnp.bfloat16).reshape(shaped)
    scores = jnp.einsum(
        "blhd,bmhd->bhlm", queries.astype(jnp.float32), keys.astype(jnp.float32)
    ) * head_dim ** (-0.5)
    positions = jnp.arange(seq_span)
    live_keys = (positions[None, None, :] <= positions[None, :, None]) & (
        positions[None, None, :] < lengths[:, None, None]
    )
    weights = (
        jnp.where(live_keys[:, None], jax.nn.silu(scores), 0.0)
        / lengths.astype(jnp.float32)[:, None, None, None]
    )
    weights = weights.astype(jnp.bfloat16)
    attended = jnp.einsum(
        "bhlm,bmhd->blhd", weights.astype(jnp.float32), values.astype(jnp.float32)
    ).reshape(samples_here * seq_span, model_width)
    mixed = (layer_norm(attended) * gate_part).astype(jnp.bfloat16)
    output = jnp.dot(mixed, w_out, preferred_element_type=jnp.float32) + embedded.reshape(
        -1, model_width
    ).astype(jnp.float32)
    return (output, mixed)


def send(src, dst, send_sem, recv_sem, **where):
    return pltpu.make_async_remote_copy(
        src_ref=src,
        dst_ref=dst,
        send_sem=send_sem,
        recv_sem=recv_sem,
        device_id=where,
        device_id_type=MESH,
    )


def each(start, stop, body):
    def step(i, carry):
        body(i)
        return carry

    lax.fori_loop(start, stop, step, 0)


def exchange_kernel(
    scale,
    outgoing,
    dense_part,
    incoming,
    table_out,
    dense_out,
    arrived,
    dense_arr,
    part,
    x_in,
    x_sum,
    y_in,
    whole,
    dx_out,
    dx_in,
    dy_in,
    d_row,
    d_all,
    z_s,
    z_r,
    dz_s,
    dz_r,
    x_s,
    x_r,
    y_s,
    y_r,
    gy_s,
    gy_r,
    gx_s,
    gx_r,
    dx_s,
    dx_r,
    dy_s,
    dy_r,
    dgx_s,
    dgx_r,
    dgz_s,
    dgz_r,
    ds_s,
    ds_r,
    side_s,
    x_mid,
    d_side,
    d_pair,
):
    nz, cap, width = outgoing.shape
    rows = table_out.shape[0]
    x_rows = rows // NX
    half = x_rows // 2
    me = lax.axis_index("table")
    spot = lax.axis_index("dp")
    x = spot // NY
    y = lax.rem(spot, NY)
    f32, bf16 = jnp.float32, jnp.bfloat16

    def zp(k):
        return lax.rem(me + k, nz)

    def xp(k):
        return lax.rem(x + k, NX)

    def yp(k):
        return lax.rem(y + k, NY)

    side = me + 1 - 2 * lax.rem(me, 2)
    x1 = x + 1 - 2 * lax.rem(x, 2)
    x2 = lax.rem(x + 2, NX)
    x3 = NX - 1 - x

    def first(c):
        return x1 + lax.rem(c, 2) * (x3 - x1)

    def second(c):
        return x3 + lax.rem(c, 2) * (x1 - x3)

    def core(k):
        return lax.rem(me + 2 * k, nz)

    def at_x(px):
        return px * NY + y

    def at_y(py):
        return x * NY + py

    barrier = pltpu.get_barrier_semaphore()

    def greet(axis, peer):
        pl.semaphore_signal(barrier, inc=1, device_id={axis: peer}, device_id_type=MESH)

    each(1, nz, lambda k: greet("table", zp(k)))
    each(1, NX, lambda k: greet("dp", at_x(xp(k))))
    each(1, NY, lambda k: greet("dp", at_y(yp(k))))
    pl.semaphore_wait(barrier, nz - 1 + NX - 1 + NY - 1)

    def z_copy(p):
        return send(outgoing.at[p], arrived.at[me], z_s.at[p], z_r.at[me], table=p)

    def z_wait(p):
        send(outgoing.at[p], arrived.at[p], z_s.at[p], z_r.at[p], table=p).wait_recv()

    def ds_copy(k):
        p = lax.rem(side + 2 * k, nz)
        return send(dense_part.at[p], d_side.at[k], ds_s.at[k], ds_r.at[k], table=side)

    def dz_copy(k):
        return send(d_pair.at[k], dense_arr.at[k], dz_s.at[k], dz_r.at[k], table=core(k))

    each(1, nz, lambda k: z_copy(zp(k)).start())
    each(0, nz // 2, lambda k: ds_copy(k).start())
    arrived[me] = outgoing[me]

    def pair_up(k):
        ds_copy(k).wait_recv()
        mine = dense_part[core(k)].astype(f32) + d_side[k].astype(f32)
        d_pair[k] = mine.astype(bf16)

    each(0, nz // 2, pair_up)
    each(1, nz, lambda k: z_wait(zp(k)))
    each(1, nz // 2, lambda k: dz_copy(k).start())

    def xa_copy(c):
        p = first(c)
        return send(part.at[p, c], x_in.at[0, c], x_s.at[0, c], x_r.at[0, c], dp=at_x(p))

    def xb_copy(c):
        p = first(c)
        return send(part.at[x2, c], x_in.at[1, c], x_s.at[1, c], x_r.at[1, c], dp=at_x(p))

    def xc_copy(c):
        p = second(c)
        return send(x_mid.at[c], x_in.at[2, c], x_s.at[2, c], x_r.at[2, c], dp=at_x(p))

    def make_part(p):
        line = lax.broadcasted_iota(jnp.int32, (x_rows, nz * cap), 0) + p * x_rows
        pick = (line == incoming[...]).astype(f32).astype(bf16)
        got = arrived[...].reshape(nz * cap, width)
        block = jnp.dot(pick, got, preferred_element_type=f32).astype(bf16)
        for c in range(NY):
            part[p, c] = block[
                (c % 2) * half : (c % 2 + 1) * half, (c // 2) * 128 : (c // 2 + 1) * 128
            ]

    def x_start(c):
        xb_copy(c).start()
        xa_copy(c).start()

    def x_middle(c):
        xb_copy(c).wait_recv()
        held = part[second(c), c].astype(f32) + x_in[1, c].astype(f32)
        x_mid[c] = held.astype(bf16)
        xc_copy(c).start()

    make_part(x2)
    make_part(x1)
    each(0, NY // 2, lambda i: x_start(2 * lax.rem(y // 2 + 1 + i, NY // 2)))
    make_part(x3)
    each(0, NY // 2, lambda i: x_start(2 * lax.rem(y // 2 + 1 + i, NY // 2) + 1))
    make_part(x)
    each(0, NY // 2, lambda i: x_middle(2 * lax.rem(y // 2 + 1 + i, NY // 2)))
    each(0, NY // 2, lambda i: x_middle(2 * lax.rem(y // 2 + 1 + i, NY // 2) + 1))

    def y_copy(c):
        return send(x_sum.at[c], y_in.at[y], y_s.at[c], y_r.at[y], dp=at_y(c))

    def y_wait(c):
        send(x_sum.at[c], y_in.at[c], y_s.at[c], y_r.at[c], dp=at_y(c)).wait_recv()

    def sum_x(c):
        xa_copy(c).wait_recv()
        xc_copy(c).wait_recv()
        total = part[x, c].astype(f32) + x_in[0, c].astype(f32) + x_in[2, c].astype(f32)
        x_sum[c] = total.astype(bf16)

    def y_stage(j):
        c = yp(j)
        sum_x(c)
        y_copy(c).start()

    each(1, NY, y_stage)
    sum_x(y)

    def dx_copy(p):
        return send(dx_out.at[p], dx_in.at[x], dx_s.at[p], dx_r.at[x], dp=at_x(p))

    def dx_wait(p):
        send(dx_out.at[p], dx_in.at[p], dx_s.at[p], dx_r.at[p], dp=at_x(p)).wait_recv()

    each(1, nz // 2, lambda k: dz_copy(k).wait_recv())
    dense_sum = d_pair[0].astype(f32)
    for k in range(1, nz // 2):
        dense_sum = dense_sum + dense_arr[k].astype(f32)
    dense_sum = dense_sum.astype(bf16)
    for c in range(NX):
        dx_out[c] = dense_sum[:, c * 128 : (c + 1) * 128]
    each(1, NX, lambda k: dx_copy(xp(k)).start())

    total = x_sum[y].astype(f32)
    for j in range(1, NY):
        c = yp(j)
        y_wait(c)
        total = total + y_in[c].astype(f32)
    whole[x, y] = total.astype(bf16)

    def gy_copy(p):
        return send(whole.at[x, y], whole.at[x, y], gy_s.at[p], gy_r.at[y], dp=at_y(p))

    def gy_wait(p):
        send(whole.at[x, p], whole.at[x, p], gy_s.at[p], gy_r.at[p], dp=at_y(p)).wait_recv()

    def gx_copy(p, c):
        return send(whole.at[x, c], whole.at[x, c], gx_s.at[p, c], gx_r.at[x, c], dp=at_x(p))

    def gx_wait(p, c):
        send(whole.at[p, c], whole.at[p, c], gx_s.at[p, c], gx_r.at[p, c], dp=at_x(p)).wait_recv()

    def gf_copy(c):
        q = second(c)
        p = first(c)
        return send(whole.at[q, c], whole.at[q, c], gx_s.at[x2, c], gx_r.at[q, c], dp=at_x(p))

    def gx_both(c):
        gx_copy(second(c), c).start()
        gx_copy(first(c), c).start()

    each(1, NY, lambda k: gy_copy(yp(k)).start())
    gx_both(y)

    def dy_copy(p):
        return send(dy_in.at[y], dy_in.at[y], dy_s.at[p], dy_r.at[y], dp=at_y(p))

    def dy_wait(p):
        send(dy_in.at[p], dy_in.at[p], dy_s.at[p], dy_r.at[p], dp=at_y(p)).wait_recv()

    dx_in[x] = dx_out[x]
    each(1, NX, lambda k: dx_wait(xp(k)))
    d_total = dx_in[0].astype(f32)
    for k in range(1, NX):
        d_total = d_total + dx_in[k].astype(f32)
    dy_in[y] = d_total.astype(bf16)
    each(1, NY, lambda k: dy_copy(yp(k)).start())

    def pass_on(j):
        c = yp(j)
        gy_wait(c)
        gx_both(c)

    each(1, NY // 2, pass_on)

    def dgx_copy(p):
        return send(d_row.at[x], d_row.at[x], dgx_s.at[p], dgx_r.at[x], dp=at_x(p))

    def dgx_wait(p):
        send(d_row.at[p], d_row.at[p], dgx_s.at[p], dgx_r.at[p], dp=at_x(p)).wait_recv()

    each(1, NY, lambda k: dy_wait(yp(k)))
    d_total = dy_in[0].astype(f32)
    for k in range(1, NY):
        d_total = d_total + dy_in[k].astype(f32)
    d_row[x] = (d_total * scale).astype(bf16)
    each(1, NX, lambda k: dgx_copy(xp(k)).start())
    each(NY // 2, NY, pass_on)

    def dgz_copy(p):
        return send(d_all.at[me], d_all.at[me], dgz_s.at[p], dgz_r.at[me], table=p)

    def dgz_wait(p):
        send(d_all.at[p], d_all.at[p], dgz_s.at[p], dgz_r.at[p], table=p).wait_recv()

    def side_copy(p):
        return send(d_all.at[p], d_all.at[p], side_s.at[p], dgz_r.at[p], table=side)

    each(1, NX, lambda k: dgx_wait(xp(k)))
    d_all[me] = d_row[...]
    each(1, nz // 2, lambda k: dgz_copy(core(k)).start())
    side_copy(me).start()

    def forward(j):
        c = yp(j)
        gx_wait(second(c), c)
        gf_copy(c).start()

    each(0, NY, forward)

    def gather_side(k):
        p = core(k)
        dgz_wait(p)
        side_copy(p).start()

    each(1, nz // 2, gather_side)

    def gx_rest(c):
        gx_wait(first(c), c)
        gx_wait(x2, c)

    each(0, NY, gx_rest)
    for px in range(NX):
        for c in range(NY):
            table_out[
                px * x_rows + (c % 2) * half : px * x_rows + (c % 2 + 1) * half,
                (c // 2) * 128 : (c // 2 + 1) * 128,
            ] = whole[px, c]
    each(0, nz // 2, lambda k: dgz_wait(lax.rem(side + 2 * k, nz)))
    for t in range(nz):
        for c in range(NX):
            dense_out[t * cap : (t + 1) * cap, c * 128 : (c + 1) * 128] = d_all[t, c]

    def sent_side(k):
        ds_copy(k).wait_send()
        side_copy(core(k)).wait_send()

    def sent_core(k):
        dz_copy(k).wait_send()
        dgz_copy(core(k)).wait_send()

    def sent_x(k):
        p = xp(k)
        dx_copy(p).wait_send()
        dgx_copy(p).wait_send()

    def sent_piece(c):
        xa_copy(c).wait_send()
        xb_copy(c).wait_send()
        xc_copy(c).wait_send()
        gx_copy(first(c), c).wait_send()
        gx_copy(second(c), c).wait_send()
        gf_copy(c).wait_send()

    def sent_y(k):
        p = yp(k)
        y_copy(p).wait_send()
        gy_copy(p).wait_send()
        dy_copy(p).wait_send()

    each(1, nz, lambda k: z_copy(zp(k)).wait_send())
    each(0, nz // 2, sent_side)
    each(1, nz // 2, sent_core)
    each(0, NY, sent_piece)
    each(1, NX, sent_x)
    each(1, NY, sent_y)


def exchange(outgoing, dense_part, incoming, shard_rows, scale):
    groups, capacity, width = outgoing.shape
    bf16 = jnp.bfloat16
    piece = (shard_rows // NX // 2, 128)
    small = (capacity, 128)
    vmem = pl.BlockSpec(memory_space=pltpu.VMEM)
    dma = pltpu.SemaphoreType.DMA

    def pair(*dims):
        return [dma(dims), dma(dims)]

    return pl.pallas_call(
        functools.partial(exchange_kernel, scale),
        out_shape=(
            jax.ShapeDtypeStruct((shard_rows, width), bf16),
            jax.ShapeDtypeStruct((groups * capacity, width), bf16),
        ),
        in_specs=[vmem] * 3,
        out_specs=(vmem, vmem),
        scratch_shapes=[
            pltpu.VMEM((groups, capacity, width), bf16),
            pltpu.VMEM((groups // 2, capacity, width), bf16),
            pltpu.VMEM((NX, NY) + piece, bf16),
            pltpu.VMEM((NX, NY) + piece, bf16),
            pltpu.VMEM((NY,) + piece, bf16),
            pltpu.VMEM((NY,) + piece, bf16),
            pltpu.VMEM((NX, NY) + piece, bf16),
            pltpu.VMEM((NX,) + small, bf16),
            pltpu.VMEM((NX,) + small, bf16),
            pltpu.VMEM((NY,) + small, bf16),
            pltpu.VMEM((NX,) + small, bf16),
            pltpu.VMEM((groups, NX) + small, bf16),
        ]
        + pair(groups)
        + pair(groups)
        + pair(NX, NY)
        + pair(NY)
        + pair(NY)
        + pair(NX, NY)
        + pair(NX)
        + pair(NY)
        + pair(NX)
        + pair(groups)
        + pair(groups // 2)
        + [
            dma((groups,)),
            pltpu.VMEM((NY,) + piece, bf16),
            pltpu.VMEM((groups // 2, capacity, width), bf16),
            pltpu.VMEM((groups // 2, capacity, width), bf16),
        ],
        compiler_params=pltpu.CompilerParams(
            collective_id=0, has_side_effects=True, vmem_limit_bytes=32 << 20
        ),
    )(outgoing, dense_part, incoming)


def dot_first(a, b):
    return lax.dot_general(a, b, (((0,), (0,)), ((), ())), preferred_element_type=jnp.float32)


def hot(shape, index):
    line = lax.broadcasted_iota(jnp.int32, shape, 0)
    return (line == index).astype(jnp.float32).astype(jnp.bfloat16)


def fetch_kernel(
    table,
    owners,
    rows,
    embedded,
    position,
    incoming,
    req_out,
    req_in,
    reply,
    got,
    q_s,
    q_r,
    r_s,
    r_r,
):
    nz, cap, width = got.shape
    slots = owners.shape[1]
    shard_rows = table.shape[0]
    per = 128 // cap
    me = lax.axis_index("table")
    f32, bf16 = jnp.float32, jnp.bfloat16

    def zp(k):
        return lax.rem(me + k, nz)

    barrier = pltpu.get_barrier_semaphore()
    each(
        1,
        nz,
        lambda k: pl.semaphore_signal(
            barrier, inc=1, device_id={"table": zp(k)}, device_id_type=MESH
        ),
    )
    own = owners[...]
    hits = (lax.broadcasted_iota(jnp.int32, (nz, slots), 0) == own).astype(f32)
    earlier = (
        lax.broadcasted_iota(jnp.int32, (slots, slots), 0)
        < lax.broadcasted_iota(jnp.int32, (slots, slots), 1)
    ).astype(f32)
    ahead = jnp.dot(hits.astype(bf16), earlier.astype(bf16), preferred_element_type=f32)
    rank = jnp.sum(hits * ahead, axis=0, keepdims=True).astype(jnp.int32)
    place = own * cap + rank
    position[...] = place
    pick = hot((nz * 128, slots), own * 128 + lax.rem(me, per) * cap + rank)
    wanted = rows[...]
    high = lax.shift_right_logical(wanted, 8)
    low = wanted & 255
    which = lax.broadcasted_iota(jnp.int32, (8, slots), 0)
    both = jnp.where(which == 0, high, jnp.where(which == 1, low, 0)).astype(f32).astype(bf16)
    found = lax.dot_general(both, pick, (((1,), (1,)), ((), ())), preferred_element_type=f32)
    asked = (found[0:1] * 256.0 + found[1:2]).astype(jnp.int32)
    for p in range(nz):
        req_out[p] = asked[:, p * 128 : (p + 1) * 128]
    pl.semaphore_wait(barrier, nz - 1)

    def q_copy(p):
        return send(req_out.at[p], req_in.at[me], q_s.at[p], q_r.at[me], table=p)

    def q_wait(p):
        send(req_out.at[p], req_in.at[p], q_s.at[p], q_r.at[p], table=p).wait_recv()

    def r_copy(p):
        return send(reply.at[p], got.at[me], r_s.at[p], r_r.at[me], table=p)

    def r_wait(p):
        send(reply.at[p], got.at[p], r_s.at[p], r_r.at[p], table=p).wait_recv()

    each(1, nz, lambda k: q_copy(zp(k)).start())
    req_in[me] = req_out[me]
    each(1, nz, lambda k: q_wait(zp(k)))
    for g in range(nz // per):
        line = req_in[g * per]
        for j in range(1, per):
            line = line + req_in[g * per + j]
        incoming[:, g * 128 : (g + 1) * 128] = line
        block = dot_first(hot((shard_rows, 128), line), table[...]).astype(bf16)
        for j in range(per):
            reply[g * per + j] = block[j * cap : (j + 1) * cap]
    each(1, nz, lambda k: r_copy(zp(k)).start())
    got[me] = reply[me]
    each(1, nz, lambda k: r_wait(zp(k)))
    spread = hot((nz * cap, slots), place)
    embedded[...] = dot_first(spread, got[...].reshape(nz * cap, width)).astype(bf16)

    def sent(k):
        q_copy(zp(k)).wait_send()
        r_copy(zp(k)).wait_send()

    each(1, nz, sent)


def fetch(table, owners, rows, groups, capacity):
    shard_rows, width = table.shape
    slots = owners.shape[1]
    vmem = pl.BlockSpec(memory_space=pltpu.VMEM)
    dma = pltpu.SemaphoreType.DMA
    return pl.pallas_call(
        fetch_kernel,
        out_shape=(
            jax.ShapeDtypeStruct((slots, width), jnp.bfloat16),
            jax.ShapeDtypeStruct((1, slots), jnp.int32),
            jax.ShapeDtypeStruct((1, groups * capacity), jnp.int32),
        ),
        in_specs=[vmem] * 3,
        out_specs=(vmem, vmem, vmem),
        scratch_shapes=[
            pltpu.VMEM((groups, 1, 128), jnp.int32),
            pltpu.VMEM((groups, 1, 128), jnp.int32),
            pltpu.VMEM((groups, capacity, width), jnp.bfloat16),
            pltpu.VMEM((groups, capacity, width), jnp.bfloat16),
            dma((groups,)),
            dma((groups,)),
            dma((groups,)),
            dma((groups,)),
        ],
        compiler_params=pltpu.CompilerParams(
            collective_id=1, has_side_effects=True, vmem_limit_bytes=32 << 20
        ),
    )(table, owners, rows)


def per_device(table, history_shard, history_row, lengths, w_in, w_out, cotangent):
    shard_rows, model_width = table.shape
    samples_here, seq_span = history_row.shape
    groups = lax.axis_size("table")
    copies = lax.axis_size("dp")
    slot_count = samples_here * seq_span
    capacity = 2 * slot_count // groups
    embedded, position, incoming = fetch(
        table,
        history_shard.reshape(1, slot_count),
        history_row.reshape(1, slot_count),
        groups,
        capacity,
    )
    slots_at = jnp.arange(groups * capacity, dtype=jnp.int32)[:, None]
    place = (slots_at == position).astype(jnp.bfloat16)
    embedded = embedded.reshape(samples_here, seq_span, model_width)
    output, pullback, mixed = jax.vjp(
        lambda rows_in: hstu_layer(rows_in, w_in, w_out, lengths), embedded, has_aux=True
    )
    row_live = jnp.arange(seq_span)[None, :] < lengths[:, None]
    grad_seed = jnp.where(row_live[:, :, None], cotangent, jnp.zeros_like(cotangent))
    flat_seed = grad_seed.reshape(-1, model_width)

    total_slots = slot_count * copies * groups
    grad_scale = 1.0 / math.sqrt(total_slots)
    dense_part = lax.dot_general(
        mixed, flat_seed, (((0,), (0,)), ((), ())), preferred_element_type=jnp.float32
    ).astype(jnp.bfloat16)
    (row_grad,) = pullback(flat_seed.astype(jnp.float32))
    outgoing = jnp.dot(
        place, row_grad.reshape(-1, model_width), preferred_element_type=jnp.float32
    ).astype(jnp.bfloat16)
    table_sum, dense_grad = exchange(
        outgoing.reshape(groups, capacity, model_width),
        dense_part.reshape(groups, capacity, model_width),
        incoming,
        shard_rows,
        grad_scale,
    )
    table_grad = table_sum.astype(jnp.float32)
    return (table_grad, dense_grad)


def solution(mesh):
    in_specs = (
        P("table", None),
        P(("dp", "table"), None, None),
        P(("dp", "table"), None),
        P(("dp", "table")),
        P(),
        P(),
        P(("dp", "table"), None, None),
    )
    out_specs = (P("table", None), P())
    return jax.shard_map(
        per_device, mesh=mesh, in_specs=in_specs, out_specs=out_specs, check_vma=False
    )
```

```python
import functools
import math

import jax
import jax.numpy as jnp
from jax import lax
from jax.experimental import pallas as pl
from jax.experimental.pallas import tpu as pltpu
from jax.sharding import PartitionSpec as P

HEADS = 4
NX = 4
NY = 8
MESH = pl.DeviceIdType.MESH


def send(src, dst, send_sem, recv_sem, **where):
    return pltpu.make_async_remote_copy(
        src_ref=src,
        dst_ref=dst,
        send_sem=send_sem,
        recv_sem=recv_sem,
        device_id=where,
        device_id_type=MESH,
    )


def each(start, stop, body):
    def step(i, carry):
        body(i)
        return carry

    lax.fori_loop(start, stop, step, 0)


def exchange_kernel(
    scale,
    outgoing,
    dense_part,
    incoming,
    table_out,
    dense_out,
    arrived,
    dense_arr,
    part,
    x_in,
    x_sum,
    y_in,
    whole,
    dx_out,
    dx_in,
    dy_in,
    d_row,
    d_all,
    z_s,
    z_r,
    dz_s,
    dz_r,
    x_s,
    x_r,
    y_s,
    y_r,
    gy_s,
    gy_r,
    gx_s,
    gx_r,
    dx_s,
    dx_r,
    dy_s,
    dy_r,
    dgx_s,
    dgx_r,
    dgz_s,
    dgz_r,
    ds_s,
    ds_r,
    side_s,
    x_mid,
    d_side,
    d_pair,
):
    nz, cap, width = outgoing.shape
    rows = table_out.shape[0]
    x_rows = rows // NX
    half = x_rows // 2
    me = lax.axis_index("table")
    spot = lax.axis_index("dp")
    x = spot // NY
    y = lax.rem(spot, NY)
    f32, bf16 = jnp.float32, jnp.bfloat16

    def zp(k):
        return lax.rem(me + k, nz)

    def xp(k):
        return lax.rem(x + k, NX)

    def yp(k):
        return lax.rem(y + k, NY)

    side = me + 1 - 2 * lax.rem(me, 2)
    x1 = x + 1 - 2 * lax.rem(x, 2)
    x2 = lax.rem(x + 2, NX)
    x3 = NX - 1 - x

    def first(c):
        return x1 + lax.rem(c, 2) * (x3 - x1)

    def second(c):
        return x3 + lax.rem(c, 2) * (x1 - x3)

    def core(k):
        return lax.rem(me + 2 * k, nz)

    def at_x(px):
        return px * NY + y

    def at_y(py):
        return x * NY + py

    barrier = pltpu.get_barrier_semaphore()

    def greet(axis, peer):
        pl.semaphore_signal(barrier, inc=1, device_id={axis: peer}, device_id_type=MESH)

    each(1, nz, lambda k: greet("table", zp(k)))
    each(1, NX, lambda k: greet("dp", at_x(xp(k))))
    each(1, NY, lambda k: greet("dp", at_y(yp(k))))
    pl.semaphore_wait(barrier, nz - 1 + NX - 1 + NY - 1)

    def z_copy(p):
        return send(outgoing.at[p], arrived.at[me], z_s.at[p], z_r.at[me], table=p)

    def z_wait(p):
        send(outgoing.at[p], arrived.at[p], z_s.at[p], z_r.at[p], table=p).wait_recv()

    def ds_copy(k):
        p = lax.rem(side + 2 * k, nz)
        return send(dense_part.at[p], d_side.at[k], ds_s.at[k], ds_r.at[k], table=side)

    def dz_copy(k):
        return send(d_pair.at[k], dense_arr.at[k], dz_s.at[k], dz_r.at[k], table=core(k))

    each(1, nz, lambda k: z_copy(zp(k)).start())
    each(0, nz // 2, lambda k: ds_copy(k).start())
    arrived[me] = outgoing[me]

    def pair_up(k):
        ds_copy(k).wait_recv()
        mine = dense_part[core(k)].astype(f32) + d_side[k].astype(f32)
        d_pair[k] = mine.astype(bf16)

    each(0, nz // 2, pair_up)
    each(1, nz, lambda k: z_wait(zp(k)))
    each(1, nz // 2, lambda k: dz_copy(k).start())

    def xa_copy(c):
        p = first(c)
        return send(part.at[p, c], x_in.at[0, c], x_s.at[0, c], x_r.at[0, c], dp=at_x(p))

    def xb_copy(c):
        p = first(c)
        return send(part.at[x2, c], x_in.at[1, c], x_s.at[1, c], x_r.at[1, c], dp=at_x(p))

    def xc_copy(c):
        p = second(c)
        return send(x_mid.at[c], x_in.at[2, c], x_s.at[2, c], x_r.at[2, c], dp=at_x(p))

    def make_part(p):
        line = lax.broadcasted_iota(jnp.int32, (x_rows, nz * cap), 0) + p * x_rows
        pick = (line == incoming[...]).astype(f32).astype(bf16)
        got = arrived[...].reshape(nz * cap, width)
        block = jnp.dot(pick, got, preferred_element_type=f32).astype(bf16)
        for c in range(NY):
            part[p, c] = block[
                (c % 2) * half : (c % 2 + 1) * half, (c // 2) * 128 : (c // 2 + 1) * 128
            ]

    def x_start(c):
        xb_copy(c).start()
        xa_copy(c).start()

    def x_middle(c):
        xb_copy(c).wait_recv()
        held = part[second(c), c].astype(f32) + x_in[1, c].astype(f32)
        x_mid[c] = held.astype(bf16)
        xc_copy(c).start()

    make_part(x2)
    make_part(x1)
    each(0, NY // 2, lambda i: x_start(2 * lax.rem(y // 2 + 1 + i, NY // 2)))
    make_part(x3)
    each(0, NY // 2, lambda i: x_start(2 * lax.rem(y // 2 + 1 + i, NY // 2) + 1))
    make_part(x)
    each(0, NY // 2, lambda i: x_middle(2 * lax.rem(y // 2 + 1 + i, NY // 2)))
    each(0, NY // 2, lambda i: x_middle(2 * lax.rem(y // 2 + 1 + i, NY // 2) + 1))

    def y_copy(c):
        return send(x_sum.at[c], y_in.at[y], y_s.at[c], y_r.at[y], dp=at_y(c))

    def y_wait(c):
        send(x_sum.at[c], y_in.at[c], y_s.at[c], y_r.at[c], dp=at_y(c)).wait_recv()

    def sum_x(c):
        xa_copy(c).wait_recv()
        xc_copy(c).wait_recv()
        total = part[x, c].astype(f32) + x_in[0, c].astype(f32) + x_in[2, c].astype(f32)
        x_sum[c] = total.astype(bf16)

    def y_stage(j):
        c = yp(j)
        sum_x(c)
        y_copy(c).start()

    each(1, NY, y_stage)
    sum_x(y)

    def dx_copy(p):
        return send(dx_out.at[p], dx_in.at[x], dx_s.at[p], dx_r.at[x], dp=at_x(p))

    def dx_wait(p):
        send(dx_out.at[p], dx_in.at[p], dx_s.at[p], dx_r.at[p], dp=at_x(p)).wait_recv()

    each(1, nz // 2, lambda k: dz_copy(k).wait_recv())
    dense_sum = d_pair[0].astype(f32)
    for k in range(1, nz // 2):
        dense_sum = dense_sum + dense_arr[k].astype(f32)
    dense_sum = dense_sum.astype(bf16)
    for c in range(NX):
        dx_out[c] = dense_sum[:, c * 128 : (c + 1) * 128]
    each(1, NX, lambda k: dx_copy(xp(k)).start())

    total = x_sum[y].astype(f32)
    for j in range(1, NY):
        c = yp(j)
        y_wait(c)
        total = total + y_in[c].astype(f32)
    whole[x, y] = total.astype(bf16)

    def gy_copy(p):
        return send(whole.at[x, y], whole.at[x, y], gy_s.at[p], gy_r.at[y], dp=at_y(p))

    def gy_wait(p):
        send(whole.at[x, p], whole.at[x, p], gy_s.at[p], gy_r.at[p], dp=at_y(p)).wait_recv()

    def gx_copy(p, c):
        return send(whole.at[x, c], whole.at[x, c], gx_s.at[p, c], gx_r.at[x, c], dp=at_x(p))

    def gx_wait(p, c):
        send(whole.at[p, c], whole.at[p, c], gx_s.at[p, c], gx_r.at[p, c], dp=at_x(p)).wait_recv()

    def gf_copy(c):
        q = second(c)
        p = first(c)
        return send(whole.at[q, c], whole.at[q, c], gx_s.at[x2, c], gx_r.at[q, c], dp=at_x(p))

    def gx_both(c):
        gx_copy(second(c), c).start()
        gx_copy(first(c), c).start()

    each(1, NY, lambda k: gy_copy(yp(k)).start())
    gx_both(y)

    def dy_copy(p):
        return send(dy_in.at[y], dy_in.at[y], dy_s.at[p], dy_r.at[y], dp=at_y(p))

    def dy_wait(p):
        send(dy_in.at[p], dy_in.at[p], dy_s.at[p], dy_r.at[p], dp=at_y(p)).wait_recv()

    dx_in[x] = dx_out[x]
    each(1, NX, lambda k: dx_wait(xp(k)))
    d_total = dx_in[0].astype(f32)
    for k in range(1, NX):
        d_total = d_total + dx_in[k].astype(f32)
    dy_in[y] = d_total.astype(bf16)
    each(1, NY, lambda k: dy_copy(yp(k)).start())

    def pass_on(j):
        c = yp(j)
        gy_wait(c)
        gx_both(c)

    each(1, NY // 2, pass_on)

    def dgx_copy(p):
        return send(d_row.at[x], d_row.at[x], dgx_s.at[p], dgx_r.at[x], dp=at_x(p))

    def dgx_wait(p):
        send(d_row.at[p], d_row.at[p], dgx_s.at[p], dgx_r.at[p], dp=at_x(p)).wait_recv()

    each(1, NY, lambda k: dy_wait(yp(k)))
    d_total = dy_in[0].astype(f32)
    for k in range(1, NY):
        d_total = d_total + dy_in[k].astype(f32)
    d_row[x] = (d_total * scale).astype(bf16)
    each(1, NX, lambda k: dgx_copy(xp(k)).start())
    each(NY // 2, NY, pass_on)

    def dgz_copy(p):
        return send(d_all.at[me], d_all.at[me], dgz_s.at[p], dgz_r.at[me], table=p)

    def dgz_wait(p):
        send(d_all.at[p], d_all.at[p], dgz_s.at[p], dgz_r.at[p], table=p).wait_recv()

    def side_copy(p):
        return send(d_all.at[p], d_all.at[p], side_s.at[p], dgz_r.at[p], table=side)

    each(1, NX, lambda k: dgx_wait(xp(k)))
    d_all[me] = d_row[...]
    each(1, nz // 2, lambda k: dgz_copy(core(k)).start())
    side_copy(me).start()

    def forward(j):
        c = yp(j)
        gx_wait(second(c), c)
        gf_copy(c).start()

    each(0, NY, forward)

    def gather_side(k):
        p = core(k)
        dgz_wait(p)
        side_copy(p).start()

    each(1, nz // 2, gather_side)

    def gx_rest(c):
        gx_wait(first(c), c)
        gx_wait(x2, c)

    each(0, NY, gx_rest)
    for px in range(NX):
        for c in range(NY):
            table_out[
                px * x_rows + (c % 2) * half : px * x_rows + (c % 2 + 1) * half,
                (c // 2) * 128 : (c // 2 + 1) * 128,
            ] = whole[px, c]
    each(0, nz // 2, lambda k: dgz_wait(lax.rem(side + 2 * k, nz)))
    for t in range(nz):
        for c in range(NX):
            dense_out[t * cap : (t + 1) * cap, c * 128 : (c + 1) * 128] = d_all[t, c]

    def sent_side(k):
        ds_copy(k).wait_send()
        side_copy(core(k)).wait_send()

    def sent_core(k):
        dz_copy(k).wait_send()
        dgz_copy(core(k)).wait_send()

    def sent_x(k):
        p = xp(k)
        dx_copy(p).wait_send()
        dgx_copy(p).wait_send()

    def sent_piece(c):
        xa_copy(c).wait_send()
        xb_copy(c).wait_send()
        xc_copy(c).wait_send()
        gx_copy(first(c), c).wait_send()
        gx_copy(second(c), c).wait_send()
        gf_copy(c).wait_send()

    def sent_y(k):
        p = yp(k)
        y_copy(p).wait_send()
        gy_copy(p).wait_send()
        dy_copy(p).wait_send()

    each(1, nz, lambda k: z_copy(zp(k)).wait_send())
    each(0, nz // 2, sent_side)
    each(1, nz // 2, sent_core)
    each(0, NY, sent_piece)
    each(1, NX, sent_x)
    each(1, NY, sent_y)


def exchange(outgoing, dense_part, incoming, shard_rows, scale):
    groups, capacity, width = outgoing.shape
    bf16 = jnp.bfloat16
    piece = (shard_rows // NX // 2, 128)
    small = (capacity, 128)
    vmem = pl.BlockSpec(memory_space=pltpu.VMEM)
    dma = pltpu.SemaphoreType.DMA

    def pair(*dims):
        return [dma(dims), dma(dims)]

    return pl.pallas_call(
        functools.partial(exchange_kernel, scale),
        out_shape=(
            jax.ShapeDtypeStruct((shard_rows, width), bf16),
            jax.ShapeDtypeStruct((groups * capacity, width), bf16),
        ),
        in_specs=[vmem] * 3,
        out_specs=(vmem, vmem),
        scratch_shapes=[
            pltpu.VMEM((groups, capacity, width), bf16),
            pltpu.VMEM((groups // 2, capacity, width), bf16),
            pltpu.VMEM((NX, NY) + piece, bf16),
            pltpu.VMEM((NX, NY) + piece, bf16),
            pltpu.VMEM((NY,) + piece, bf16),
            pltpu.VMEM((NY,) + piece, bf16),
            pltpu.VMEM((NX, NY) + piece, bf16),
            pltpu.VMEM((NX,) + small, bf16),
            pltpu.VMEM((NX,) + small, bf16),
            pltpu.VMEM((NY,) + small, bf16),
            pltpu.VMEM((NX,) + small, bf16),
            pltpu.VMEM((groups, NX) + small, bf16),
        ]
        + pair(groups)
        + pair(groups)
        + pair(NX, NY)
        + pair(NY)
        + pair(NY)
        + pair(NX, NY)
        + pair(NX)
        + pair(NY)
        + pair(NX)
        + pair(groups)
        + pair(groups // 2)
        + [
            dma((groups,)),
            pltpu.VMEM((NY,) + piece, bf16),
            pltpu.VMEM((groups // 2, capacity, width), bf16),
            pltpu.VMEM((groups // 2, capacity, width), bf16),
        ],
        compiler_params=pltpu.CompilerParams(
            collective_id=0, has_side_effects=True, vmem_limit_bytes=32 << 20
        ),
    )(outgoing, dense_part, incoming)


def dot_first(a, b):
    return lax.dot_general(a, b, (((0,), (0,)), ((), ())), preferred_element_type=jnp.float32)


def hot(shape, index):
    line = lax.broadcasted_iota(jnp.int32, shape, 0)
    return (line == index).astype(jnp.float32).astype(jnp.bfloat16)


def fetch_kernel(
    table,
    owners,
    rows,
    embedded,
    position,
    incoming,
    req_out,
    req_in,
    reply,
    got,
    q_s,
    q_r,
    r_s,
    r_r,
):
    nz, cap, width = got.shape
    slots = owners.shape[1]
    shard_rows = table.shape[0]
    per = 128 // cap
    me = lax.axis_index("table")
    f32, bf16 = jnp.float32, jnp.bfloat16

    def zp(k):
        return lax.rem(me + k, nz)

    barrier = pltpu.get_barrier_semaphore()
    each(
        1,
        nz,
        lambda k: pl.semaphore_signal(
            barrier, inc=1, device_id={"table": zp(k)}, device_id_type=MESH
        ),
    )
    own = owners[...]
    hits = (lax.broadcasted_iota(jnp.int32, (nz, slots), 0) == own).astype(f32)
    earlier = (
        lax.broadcasted_iota(jnp.int32, (slots, slots), 0)
        < lax.broadcasted_iota(jnp.int32, (slots, slots), 1)
    ).astype(f32)
    ahead = jnp.dot(hits.astype(bf16), earlier.astype(bf16), preferred_element_type=f32)
    rank = jnp.sum(hits * ahead, axis=0, keepdims=True).astype(jnp.int32)
    place = own * cap + rank
    position[...] = place
    pick = hot((nz * 128, slots), own * 128 + lax.rem(me, per) * cap + rank)
    wanted = rows[...]
    high = lax.shift_right_logical(wanted, 8)
    low = wanted & 255
    which = lax.broadcasted_iota(jnp.int32, (8, slots), 0)
    both = jnp.where(which == 0, high, jnp.where(which == 1, low, 0)).astype(f32).astype(bf16)
    found = lax.dot_general(both, pick, (((1,), (1,)), ((), ())), preferred_element_type=f32)
    asked = (found[0:1] * 256.0 + found[1:2]).astype(jnp.int32)
    for p in range(nz):
        req_out[p] = asked[:, p * 128 : (p + 1) * 128]
    pl.semaphore_wait(barrier, nz - 1)

    def q_copy(p):
        return send(req_out.at[p], req_in.at[me], q_s.at[p], q_r.at[me], table=p)

    def q_wait(p):
        send(req_out.at[p], req_in.at[p], q_s.at[p], q_r.at[p], table=p).wait_recv()

    def r_copy(p):
        return send(reply.at[p], got.at[me], r_s.at[p], r_r.at[me], table=p)

    def r_wait(p):
        send(reply.at[p], got.at[p], r_s.at[p], r_r.at[p], table=p).wait_recv()

    each(1, nz, lambda k: q_copy(zp(k)).start())
    req_in[me] = req_out[me]
    each(1, nz, lambda k: q_wait(zp(k)))
    for g in range(nz // per):
        line = req_in[g * per]
        for j in range(1, per):
            line = line + req_in[g * per + j]
        incoming[:, g * 128 : (g + 1) * 128] = line
        block = dot_first(hot((shard_rows, 128), line), table[...]).astype(bf16)
        for j in range(per):
            reply[g * per + j] = block[j * cap : (j + 1) * cap]
    each(1, nz, lambda k: r_copy(zp(k)).start())
    got[me] = reply[me]
    each(1, nz, lambda k: r_wait(zp(k)))
    spread = hot((nz * cap, slots), place)
    embedded[...] = dot_first(spread, got[...].reshape(nz * cap, width)).astype(bf16)

    def sent(k):
        q_copy(zp(k)).wait_send()
        r_copy(zp(k)).wait_send()

    each(1, nz, sent)


def fetch(table, owners, rows, groups, capacity):
    shard_rows, width = table.shape
    slots = owners.shape[1]
    vmem = pl.BlockSpec(memory_space=pltpu.VMEM)
    dma = pltpu.SemaphoreType.DMA
    return pl.pallas_call(
        fetch_kernel,
        out_shape=(
            jax.ShapeDtypeStruct((slots, width), jnp.bfloat16),
            jax.ShapeDtypeStruct((1, slots), jnp.int32),
            jax.ShapeDtypeStruct((1, groups * capacity), jnp.int32),
        ),
        in_specs=[vmem] * 3,
        out_specs=(vmem, vmem, vmem),
        scratch_shapes=[
            pltpu.VMEM((groups, 1, 128), jnp.int32),
            pltpu.VMEM((groups, 1, 128), jnp.int32),
            pltpu.VMEM((groups, capacity, width), jnp.bfloat16),
            pltpu.VMEM((groups, capacity, width), jnp.bfloat16),
            dma((groups,)),
            dma((groups,)),
            dma((groups,)),
            dma((groups,)),
        ],
        compiler_params=pltpu.CompilerParams(
            collective_id=1, has_side_effects=True, vmem_limit_bytes=32 << 20
        ),
    )(table, owners, rows)


def centre(values):
    shifted = values - jnp.mean(values, axis=-1, keepdims=True)
    spread = lax.rsqrt(jnp.mean(shifted * shifted, axis=-1, keepdims=True) + 1e-06)
    return shifted * spread, spread


def centre_back(grad, unit, spread):
    along = jnp.mean(grad * unit, axis=-1, keepdims=True)
    return spread * (grad - jnp.mean(grad, axis=-1, keepdims=True) - unit * along)


def dot_last(a, b):
    return lax.dot_general(a, b, (((1,), (1,)), ((), ())), preferred_element_type=jnp.float32)


def dot_plain(a, b):
    return jnp.dot(a, b, preferred_element_type=jnp.float32)


def layer_kernel(
    lengths, embedded, position, w_in, w_out, cotangent, outgoing, dense_part, before, after, grad
):
    f32, bf16 = jnp.float32, jnp.bfloat16
    span, width = embedded.shape
    head = width // HEADS
    length = lengths[0]
    share = 1.0 / length.astype(f32)
    unit, spread = centre(embedded[...].astype(f32))
    normed = unit.astype(bf16)
    for b in range(4):
        cols = slice(b * width, (b + 1) * width)
        made = dot_plain(normed, w_in[:, cols])
        before[:, cols] = made
        if b > 0:
            after[:, cols] = (made * jax.nn.sigmoid(made)).astype(bf16)
    row = lax.broadcasted_iota(jnp.int32, (span, span), 0)
    col = lax.broadcasted_iota(jnp.int32, (span, span), 1)
    live = (col <= row) & (col < length)
    scale = head ** (-0.5)

    def columns(part, h):
        return slice(part * width + h * head, part * width + (h + 1) * head)

    attended = []
    kept = []
    for h in range(HEADS):
        scores = dot_last(after[:, columns(2, h)], after[:, columns(3, h)]) * scale
        gain = jax.nn.sigmoid(scores)
        weights = (jnp.where(live, scores * gain, 0.0) * share).astype(bf16)
        slope = jnp.where(live, gain * (1.0 + scores * (1.0 - gain)), 0.0) * share
        attended.append(dot_plain(weights, after[:, columns(1, h)]))
        kept.append((weights, slope))
    mid, mid_spread = centre(jnp.concatenate(attended, axis=1))
    gate_in = before[:, :width]
    gate_sig = jax.nn.sigmoid(gate_in)
    gate = gate_in * gate_sig
    mixed = (mid * gate).astype(bf16)
    item = lax.broadcasted_iota(jnp.int32, (span, width), 0)
    seed = jnp.where(item < length, cotangent[...].astype(f32), 0.0)
    seed_low = seed.astype(bf16)
    dense_part[...] = dot_first(mixed, seed_low).astype(bf16)

    d_mixed = dot_last(seed_low, w_out[...]).astype(bf16).astype(f32)
    grad[:, :width] = (d_mixed * mid * (gate_sig * (1.0 + gate_in * (1.0 - gate_sig)))).astype(bf16)
    d_att = centre_back(d_mixed * gate, mid, mid_spread).astype(bf16)

    def keep(part, h, value):
        cols = columns(part, h)
        x = before[:, cols]
        sig = jax.nn.sigmoid(x)
        grad[:, cols] = (value * (sig * (1.0 + x * (1.0 - sig)))).astype(bf16)

    for h in range(HEADS):
        weights, slope = kept[h]
        d_head = d_att[:, h * head : (h + 1) * head]
        d_scores = (dot_last(d_head, after[:, columns(1, h)]) * slope * scale).astype(bf16)
        keep(1, h, dot_first(weights, d_head))
        keep(2, h, dot_plain(d_scores, after[:, columns(3, h)]))
        keep(3, h, dot_first(d_scores, after[:, columns(2, h)]))
    d_normed = dot_last(grad[:, :width], w_in[:, :width])
    for b in range(1, 4):
        cols = slice(b * width, (b + 1) * width)
        d_normed = d_normed + dot_last(grad[:, cols], w_in[:, cols])
    row_grad = (centre_back(d_normed, unit, spread) + seed).astype(bf16)
    spots = hot((outgoing.shape[0], span), position[...])
    outgoing[...] = dot_plain(spots, row_grad).astype(bf16)


def layer(lengths, embedded, position, w_in, w_out, cotangent, spots):
    span, width = embedded.shape
    vmem = pl.BlockSpec(memory_space=pltpu.VMEM)
    return pl.pallas_call(
        layer_kernel,
        out_shape=(
            jax.ShapeDtypeStruct((spots, width), jnp.bfloat16),
            jax.ShapeDtypeStruct((width, width), jnp.bfloat16),
        ),
        in_specs=[pl.BlockSpec(memory_space=pltpu.SMEM)] + [vmem] * 5,
        out_specs=(vmem, vmem),
        scratch_shapes=[
            pltpu.VMEM((span, 4 * width), jnp.float32),
            pltpu.VMEM((span, 4 * width), jnp.bfloat16),
            pltpu.VMEM((span, 4 * width), jnp.bfloat16),
        ],
        compiler_params=pltpu.CompilerParams(vmem_limit_bytes=40 << 20),
    )(lengths, embedded, position, w_in, w_out, cotangent)


def per_device(table, history_shard, history_row, lengths, w_in, w_out, cotangent):
    shard_rows, model_width = table.shape
    samples_here, seq_span = history_row.shape
    groups = lax.axis_size("table")
    copies = lax.axis_size("dp")
    slot_count = samples_here * seq_span
    capacity = 2 * slot_count // groups
    embedded, position, incoming = fetch(
        table,
        history_shard.reshape(1, slot_count),
        history_row.reshape(1, slot_count),
        groups,
        capacity,
    )
    outgoing, dense_part = layer(
        lengths,
        embedded,
        position,
        w_in,
        w_out,
        cotangent.reshape(slot_count, model_width),
        groups * capacity,
    )
    total_slots = slot_count * copies * groups
    grad_scale = 1.0 / math.sqrt(total_slots)
    table_sum, dense_grad = exchange(
        outgoing.reshape(groups, capacity, model_width),
        dense_part.reshape(groups, capacity, model_width),
        incoming,
        shard_rows,
        grad_scale,
    )
    table_grad = table_sum.astype(jnp.float32)
    return (table_grad, dense_grad)


def solution(mesh):
    in_specs = (
        P("table", None),
        P(("dp", "table"), None, None),
        P(("dp", "table"), None),
        P(("dp", "table")),
        P(),
        P(),
        P(("dp", "table"), None, None),
    )
    out_specs = (P("table", None), P())
    return jax.shard_map(
        per_device, mesh=mesh, in_specs=in_specs, out_specs=out_specs, check_vma=False
    )
```

```python
import functools
import math

import jax
import jax.numpy as jnp
from jax import lax
from jax.experimental import pallas as pl
from jax.experimental.pallas import tpu as pltpu
from jax.sharding import PartitionSpec as P

HEADS = 4
NX = 4
NY = 8
MESH = pl.DeviceIdType.MESH


def send(src, dst, send_sem, recv_sem, **where):
    return pltpu.make_async_remote_copy(
        src_ref=src,
        dst_ref=dst,
        send_sem=send_sem,
        recv_sem=recv_sem,
        device_id=where,
        device_id_type=MESH,
    )


def each(start, stop, body):
    def step(i, carry):
        body(i)
        return carry

    lax.fori_loop(start, stop, step, 0)


def exchange_kernel(
    scale,
    outgoing,
    dense_part,
    incoming,
    table_out,
    dense_out,
    arrived,
    dense_arr,
    part,
    x_in,
    x_sum,
    y_in,
    whole,
    dx_out,
    dx_in,
    dy_in,
    d_row,
    d_all,
    z_s,
    z_r,
    dz_s,
    dz_r,
    x_s,
    x_r,
    y_s,
    y_r,
    gy_s,
    gy_r,
    gx_s,
    gx_r,
    dx_s,
    dx_r,
    dy_s,
    dy_r,
    dgx_s,
    dgx_r,
    dgz_s,
    dgz_r,
    ds_s,
    ds_r,
    side_s,
    x_mid,
    d_side,
    d_pair,
):
    nz, cap, width = outgoing.shape
    rows = table_out.shape[0]
    x_rows = rows // NX
    half = x_rows // 2
    me = lax.axis_index("table")
    spot = lax.axis_index("dp")
    x = spot // NY
    y = lax.rem(spot, NY)
    f32, bf16 = jnp.float32, jnp.bfloat16

    def zp(k):
        return lax.rem(me + k, nz)

    def xp(k):
        return lax.rem(x + k, NX)

    def yp(k):
        return lax.rem(y + k, NY)

    side = me + 1 - 2 * lax.rem(me, 2)
    x1 = x + 1 - 2 * lax.rem(x, 2)
    x2 = lax.rem(x + 2, NX)
    x3 = NX - 1 - x

    def first(c):
        return x1 + lax.rem(c, 2) * (x3 - x1)

    def second(c):
        return x3 + lax.rem(c, 2) * (x1 - x3)

    def core(k):
        return lax.rem(me + 2 * k, nz)

    def at_x(px):
        return px * NY + y

    def at_y(py):
        return x * NY + py

    def z_copy(p):
        return send(outgoing.at[p], arrived.at[me], z_s.at[p], z_r.at[me], table=p)

    def z_wait(p):
        send(outgoing.at[p], arrived.at[p], z_s.at[p], z_r.at[p], table=p).wait_recv()

    def ds_copy(k):
        p = lax.rem(side + 2 * k, nz)
        return send(dense_part.at[p], d_side.at[k], ds_s.at[k], ds_r.at[k], table=side)

    def dz_copy(k):
        return send(d_pair.at[k], dense_arr.at[k], dz_s.at[k], dz_r.at[k], table=core(k))

    each(1, nz, lambda k: z_copy(zp(k)).start())
    each(0, nz // 2, lambda k: ds_copy(k).start())
    arrived[me] = outgoing[me]

    def pair_up(k):
        ds_copy(k).wait_recv()
        mine = dense_part[core(k)].astype(f32) + d_side[k].astype(f32)
        d_pair[k] = mine.astype(bf16)

    each(0, nz // 2, pair_up)
    each(1, nz, lambda k: z_wait(zp(k)))
    each(1, nz // 2, lambda k: dz_copy(k).start())

    def xa_copy(c):
        p = first(c)
        return send(part.at[p, c], x_in.at[0, c], x_s.at[0, c], x_r.at[0, c], dp=at_x(p))

    def xb_copy(c):
        p = first(c)
        return send(part.at[x2, c], x_in.at[1, c], x_s.at[1, c], x_r.at[1, c], dp=at_x(p))

    def xc_copy(c):
        p = second(c)
        return send(x_mid.at[c], x_in.at[2, c], x_s.at[2, c], x_r.at[2, c], dp=at_x(p))

    def make_part(p):
        line = lax.broadcasted_iota(jnp.int32, (x_rows, nz * cap), 0) + p * x_rows
        pick = (line == incoming[...]).astype(f32).astype(bf16)
        got = arrived[...].reshape(nz * cap, width)
        block = jnp.dot(pick, got, preferred_element_type=f32).astype(bf16)
        for c in range(NY):
            part[p, c] = block[
                (c % 2) * half : (c % 2 + 1) * half, (c // 2) * 128 : (c // 2 + 1) * 128
            ]

    def x_start(c):
        xb_copy(c).start()
        xa_copy(c).start()

    def x_middle(c):
        xb_copy(c).wait_recv()
        held = part[second(c), c].astype(f32) + x_in[1, c].astype(f32)
        x_mid[c] = held.astype(bf16)
        xc_copy(c).start()

    make_part(x2)
    make_part(x1)
    each(0, NY // 2, lambda i: x_start(2 * lax.rem(y // 2 + 1 + i, NY // 2)))
    make_part(x3)
    each(0, NY // 2, lambda i: x_start(2 * lax.rem(y // 2 + 1 + i, NY // 2) + 1))
    make_part(x)
    each(0, NY // 2, lambda i: x_middle(2 * lax.rem(y // 2 + 1 + i, NY // 2)))
    each(0, NY // 2, lambda i: x_middle(2 * lax.rem(y // 2 + 1 + i, NY // 2) + 1))

    def y_copy(c):
        return send(x_sum.at[c], y_in.at[y], y_s.at[c], y_r.at[y], dp=at_y(c))

    def y_wait(c):
        send(x_sum.at[c], y_in.at[c], y_s.at[c], y_r.at[c], dp=at_y(c)).wait_recv()

    def sum_x(c):
        xa_copy(c).wait_recv()
        xc_copy(c).wait_recv()
        total = part[x, c].astype(f32) + x_in[0, c].astype(f32) + x_in[2, c].astype(f32)
        x_sum[c] = total.astype(bf16)

    def y_stage(j):
        c = yp(j)
        sum_x(c)
        y_copy(c).start()

    each(1, NY, y_stage)
    sum_x(y)

    def dx_copy(p):
        return send(dx_out.at[p], dx_in.at[x], dx_s.at[p], dx_r.at[x], dp=at_x(p))

    def dx_wait(p):
        send(dx_out.at[p], dx_in.at[p], dx_s.at[p], dx_r.at[p], dp=at_x(p)).wait_recv()

    each(1, nz // 2, lambda k: dz_copy(k).wait_recv())
    dense_sum = d_pair[0].astype(f32)
    for k in range(1, nz // 2):
        dense_sum = dense_sum + dense_arr[k].astype(f32)
    dense_sum = dense_sum.astype(bf16)
    for c in range(NX):
        dx_out[c] = dense_sum[:, c * 128 : (c + 1) * 128]
    each(1, NX, lambda k: dx_copy(xp(k)).start())

    total = x_sum[y].astype(f32)
    for j in range(1, NY):
        c = yp(j)
        y_wait(c)
        total = total + y_in[c].astype(f32)
    whole[x, y] = total.astype(bf16)

    def gy_copy(p):
        return send(whole.at[x, y], whole.at[x, y], gy_s.at[p], gy_r.at[y], dp=at_y(p))

    def gy_wait(p):
        send(whole.at[x, p], whole.at[x, p], gy_s.at[p], gy_r.at[p], dp=at_y(p)).wait_recv()

    def gx_copy(p, c):
        return send(whole.at[x, c], whole.at[x, c], gx_s.at[p, c], gx_r.at[x, c], dp=at_x(p))

    def gx_wait(p, c):
        send(whole.at[p, c], whole.at[p, c], gx_s.at[p, c], gx_r.at[p, c], dp=at_x(p)).wait_recv()

    def gf_copy(c):
        q = second(c)
        p = first(c)
        return send(whole.at[q, c], whole.at[q, c], gx_s.at[x2, c], gx_r.at[q, c], dp=at_x(p))

    def gx_both(c):
        gx_copy(second(c), c).start()
        gx_copy(first(c), c).start()

    each(1, NY, lambda k: gy_copy(yp(k)).start())
    gx_both(y)

    def dy_copy(p):
        return send(dy_in.at[y], dy_in.at[y], dy_s.at[p], dy_r.at[y], dp=at_y(p))

    def dy_wait(p):
        send(dy_in.at[p], dy_in.at[p], dy_s.at[p], dy_r.at[p], dp=at_y(p)).wait_recv()

    dx_in[x] = dx_out[x]
    each(1, NX, lambda k: dx_wait(xp(k)))
    d_total = dx_in[0].astype(f32)
    for k in range(1, NX):
        d_total = d_total + dx_in[k].astype(f32)
    dy_in[y] = d_total.astype(bf16)
    each(1, NY, lambda k: dy_copy(yp(k)).start())

    def pass_on(j):
        c = yp(j)
        gy_wait(c)
        gx_both(c)

    each(1, NY // 2, pass_on)

    def dgx_copy(p):
        return send(d_row.at[x], d_row.at[x], dgx_s.at[p], dgx_r.at[x], dp=at_x(p))

    def dgx_wait(p):
        send(d_row.at[p], d_row.at[p], dgx_s.at[p], dgx_r.at[p], dp=at_x(p)).wait_recv()

    each(1, NY, lambda k: dy_wait(yp(k)))
    d_total = dy_in[0].astype(f32)
    for k in range(1, NY):
        d_total = d_total + dy_in[k].astype(f32)
    d_row[x] = (d_total * scale).astype(bf16)
    each(1, NX, lambda k: dgx_copy(xp(k)).start())
    each(NY // 2, NY, pass_on)

    def dgz_copy(p):
        return send(d_all.at[me], d_all.at[me], dgz_s.at[p], dgz_r.at[me], table=p)

    def dgz_wait(p):
        send(d_all.at[p], d_all.at[p], dgz_s.at[p], dgz_r.at[p], table=p).wait_recv()

    def side_copy(p):
        return send(d_all.at[p], d_all.at[p], side_s.at[p], dgz_r.at[p], table=side)

    each(1, NX, lambda k: dgx_wait(xp(k)))
    d_all[me] = d_row[...]
    each(1, nz // 2, lambda k: dgz_copy(core(k)).start())
    side_copy(me).start()

    def forward(j):
        c = yp(j)
        gx_wait(second(c), c)
        gf_copy(c).start()

    each(0, NY, forward)

    def gather_side(k):
        p = core(k)
        dgz_wait(p)
        side_copy(p).start()

    each(1, nz // 2, gather_side)

    def gx_rest(c):
        gx_wait(first(c), c)
        gx_wait(x2, c)

    each(0, NY, gx_rest)
    for px in range(NX):
        for c in range(NY):
            table_out[
                px * x_rows + (c % 2) * half : px * x_rows + (c % 2 + 1) * half,
                (c // 2) * 128 : (c // 2 + 1) * 128,
            ] = whole[px, c]
    each(0, nz // 2, lambda k: dgz_wait(lax.rem(side + 2 * k, nz)))
    for t in range(nz):
        for c in range(NX):
            dense_out[t * cap : (t + 1) * cap, c * 128 : (c + 1) * 128] = d_all[t, c]

    def sent_side(k):
        ds_copy(k).wait_send()
        side_copy(core(k)).wait_send()

    def sent_core(k):
        dz_copy(k).wait_send()
        dgz_copy(core(k)).wait_send()

    def sent_x(k):
        p = xp(k)
        dx_copy(p).wait_send()
        dgx_copy(p).wait_send()

    def sent_piece(c):
        xa_copy(c).wait_send()
        xb_copy(c).wait_send()
        xc_copy(c).wait_send()
        gx_copy(first(c), c).wait_send()
        gx_copy(second(c), c).wait_send()
        gf_copy(c).wait_send()

    def sent_y(k):
        p = yp(k)
        y_copy(p).wait_send()
        gy_copy(p).wait_send()
        dy_copy(p).wait_send()

    each(1, nz, lambda k: z_copy(zp(k)).wait_send())
    each(0, nz // 2, sent_side)
    each(1, nz // 2, sent_core)
    each(0, NY, sent_piece)
    each(1, NX, sent_x)
    each(1, NY, sent_y)


def dot_first(a, b):
    return lax.dot_general(a, b, (((0,), (0,)), ((), ())), preferred_element_type=jnp.float32)


def hot(shape, index):
    line = lax.broadcasted_iota(jnp.int32, shape, 0)
    return (line == index).astype(jnp.float32).astype(jnp.bfloat16)


def fetch_kernel(
    ready,
    table_here,
    table,
    owners,
    rows,
    embedded,
    position,
    incoming,
    req_out,
    req_in,
    reply,
    got,
    q_s,
    q_r,
    r_s,
    r_r,
):
    nz, cap, width = got.shape
    slots = owners.shape[1]
    shard_rows = table.shape[0]
    per = 128 // cap
    me = lax.axis_index("table")
    f32, bf16 = jnp.float32, jnp.bfloat16

    def zp(k):
        return lax.rem(me + k, nz)

    own = owners[...]
    hits = (lax.broadcasted_iota(jnp.int32, (nz, slots), 0) == own).astype(f32)
    earlier = (
        lax.broadcasted_iota(jnp.int32, (slots, slots), 0)
        < lax.broadcasted_iota(jnp.int32, (slots, slots), 1)
    ).astype(f32)
    ahead = jnp.dot(hits.astype(bf16), earlier.astype(bf16), preferred_element_type=f32)
    rank = jnp.sum(hits * ahead, axis=0, keepdims=True).astype(jnp.int32)
    place = own * cap + rank
    position[...] = place
    pick = hot((nz * 128, slots), own * 128 + lax.rem(me, per) * cap + rank)
    wanted = rows[...]
    high = lax.shift_right_logical(wanted, 8)
    low = wanted & 255
    which = lax.broadcasted_iota(jnp.int32, (8, slots), 0)
    both = jnp.where(which == 0, high, jnp.where(which == 1, low, 0)).astype(f32).astype(bf16)
    found = lax.dot_general(both, pick, (((1,), (1,)), ((), ())), preferred_element_type=f32)
    asked = (found[0:1] * 256.0 + found[1:2]).astype(jnp.int32)
    for p in range(nz):
        req_out[p] = asked[:, p * 128 : (p + 1) * 128]
    ready()

    def q_copy(p):
        return send(req_out.at[p], req_in.at[me], q_s.at[p], q_r.at[me], table=p)

    def q_wait(p):
        send(req_out.at[p], req_in.at[p], q_s.at[p], q_r.at[p], table=p).wait_recv()

    def r_copy(p):
        return send(reply.at[p], got.at[me], r_s.at[p], r_r.at[me], table=p)

    def r_wait(p):
        send(reply.at[p], got.at[p], r_s.at[p], r_r.at[p], table=p).wait_recv()

    each(1, nz, lambda k: q_copy(zp(k)).start())
    req_in[me] = req_out[me]
    each(1, nz, lambda k: q_wait(zp(k)))
    table_here()
    for g in range(nz // per):
        line = req_in[g * per]
        for j in range(1, per):
            line = line + req_in[g * per + j]
        incoming[:, g * 128 : (g + 1) * 128] = line
        block = dot_first(hot((shard_rows, 128), line), table[...]).astype(bf16)
        for j in range(per):
            reply[g * per + j] = block[j * cap : (j + 1) * cap]
    each(1, nz, lambda k: r_copy(zp(k)).start())
    got[me] = reply[me]
    each(1, nz, lambda k: r_wait(zp(k)))
    spread = hot((nz * cap, slots), place)
    embedded[...] = dot_first(spread, got[...].reshape(nz * cap, width)).astype(bf16)

    def sent(k):
        q_copy(zp(k)).wait_send()
        r_copy(zp(k)).wait_send()

    each(1, nz, sent)


def centre(values):
    shifted = values - jnp.mean(values, axis=-1, keepdims=True)
    spread = lax.rsqrt(jnp.mean(shifted * shifted, axis=-1, keepdims=True) + 1e-06)
    return shifted * spread, spread


def centre_back(grad, unit, spread):
    along = jnp.mean(grad * unit, axis=-1, keepdims=True)
    return spread * (grad - jnp.mean(grad, axis=-1, keepdims=True) - unit * along)


def dot_last(a, b):
    return lax.dot_general(a, b, (((1,), (1,)), ((), ())), preferred_element_type=jnp.float32)


def dot_plain(a, b):
    return jnp.dot(a, b, preferred_element_type=jnp.float32)


def layer_kernel(
    lengths, embedded, position, w_in, w_out, cotangent, outgoing, dense_part, before, after, grad
):
    f32, bf16 = jnp.float32, jnp.bfloat16
    span, width = embedded.shape
    head = width // HEADS
    length = lengths[0]
    share = 1.0 / length.astype(f32)
    unit, spread = centre(embedded[...].astype(f32))
    normed = unit.astype(bf16)
    for b in range(4):
        cols = slice(b * width, (b + 1) * width)
        made = dot_plain(normed, w_in[:, cols])
        before[:, cols] = made
        if b > 0:
            after[:, cols] = (made * jax.nn.sigmoid(made)).astype(bf16)
    row = lax.broadcasted_iota(jnp.int32, (span, span), 0)
    col = lax.broadcasted_iota(jnp.int32, (span, span), 1)
    live = (col <= row) & (col < length)
    scale = head ** (-0.5)

    def columns(part, h):
        return slice(part * width + h * head, part * width + (h + 1) * head)

    attended = []
    kept = []
    for h in range(HEADS):
        scores = dot_last(after[:, columns(2, h)], after[:, columns(3, h)]) * scale
        gain = jax.nn.sigmoid(scores)
        weights = (jnp.where(live, scores * gain, 0.0) * share).astype(bf16)
        slope = jnp.where(live, gain * (1.0 + scores * (1.0 - gain)), 0.0) * share
        attended.append(dot_plain(weights, after[:, columns(1, h)]))
        kept.append((weights, slope))
    mid, mid_spread = centre(jnp.concatenate(attended, axis=1))
    gate_in = before[:, :width]
    gate_sig = jax.nn.sigmoid(gate_in)
    gate = gate_in * gate_sig
    mixed = (mid * gate).astype(bf16)
    item = lax.broadcasted_iota(jnp.int32, (span, width), 0)
    seed = jnp.where(item < length, cotangent[...].astype(f32), 0.0)
    seed_low = seed.astype(bf16)
    dense_part[...] = dot_first(mixed, seed_low).astype(bf16).reshape(dense_part.shape)

    d_mixed = dot_last(seed_low, w_out[...]).astype(bf16).astype(f32)
    grad[:, :width] = (d_mixed * mid * (gate_sig * (1.0 + gate_in * (1.0 - gate_sig)))).astype(bf16)
    d_att = centre_back(d_mixed * gate, mid, mid_spread).astype(bf16)

    def keep(part, h, value):
        cols = columns(part, h)
        x = before[:, cols]
        sig = jax.nn.sigmoid(x)
        grad[:, cols] = (value * (sig * (1.0 + x * (1.0 - sig)))).astype(bf16)

    for h in range(HEADS):
        weights, slope = kept[h]
        d_head = d_att[:, h * head : (h + 1) * head]
        d_scores = (dot_last(d_head, after[:, columns(1, h)]) * slope * scale).astype(bf16)
        keep(1, h, dot_first(weights, d_head))
        keep(2, h, dot_plain(d_scores, after[:, columns(3, h)]))
        keep(3, h, dot_first(d_scores, after[:, columns(2, h)]))
    d_normed = dot_last(grad[:, :width], w_in[:, :width])
    for b in range(1, 4):
        cols = slice(b * width, (b + 1) * width)
        d_normed = d_normed + dot_last(grad[:, cols], w_in[:, cols])
    row_grad = (centre_back(d_normed, unit, spread) + seed).astype(bf16)
    nz, cap, _ = outgoing.shape
    spots = hot((nz * cap, span), position[...])
    outgoing[...] = dot_plain(spots, row_grad).astype(bf16).reshape(outgoing.shape)


def step_kernel(
    scale,
    lengths,
    table_far,
    owners,
    rows,
    w_in_far,
    w_out_far,
    cotangent_far,
    table_out,
    dense_out,
    table,
    w_in,
    w_out,
    cotangent,
    near_s,
    embedded,
    position,
    incoming,
    outgoing,
    dense_part,
    *scratch,
):
    nz = outgoing.shape[0]
    me = lax.axis_index("table")
    spot = lax.axis_index("dp")
    x = spot // NY
    y = lax.rem(spot, NY)
    barrier = pltpu.get_barrier_semaphore()

    def greet(axis, peer):
        pl.semaphore_signal(barrier, inc=1, device_id={axis: peer}, device_id_type=MESH)

    each(1, nz, lambda k: greet("table", lax.rem(me + k, nz)))
    each(1, NX, lambda k: greet("dp", lax.rem(x + k, NX) * NY + y))
    each(1, NY, lambda k: greet("dp", x * NY + lax.rem(y + k, NY)))

    pairs = ((table_far, table), (w_in_far, w_in), (w_out_far, w_out), (cotangent_far, cotangent))
    copies = [pltpu.make_async_copy(a, b, near_s.at[i]) for i, (a, b) in enumerate(pairs)]
    for copy in copies:
        copy.start()

    def ready():
        pl.semaphore_wait(barrier, nz - 1 + NX - 1 + NY - 1)

    fetch_kernel(
        ready, copies[0].wait, table, owners, rows, embedded, position, incoming, *scratch[:8]
    )
    for copy in copies[1:]:
        copy.wait()
    layer_kernel(
        lengths,
        embedded,
        position,
        w_in,
        w_out,
        cotangent,
        outgoing,
        dense_part,
        *scratch[8:11],
    )
    exchange_kernel(
        scale, outgoing, dense_part, incoming, table_out, dense_out, *scratch[11:]
    )


def step(lengths, table, owners, rows, w_in, w_out, cotangent, groups, capacity, scale):
    shard_rows, width = table.shape
    slots = owners.shape[1]
    bf16, f32, i32 = jnp.bfloat16, jnp.float32, jnp.int32
    piece = (shard_rows // NX // 2, 128)
    small = (capacity, 128)
    block = (groups, capacity, width)
    vmem = pl.BlockSpec(memory_space=pltpu.VMEM)
    far = pl.BlockSpec(memory_space=pl.ANY)
    dma = pltpu.SemaphoreType.DMA
    room = pltpu.VMEM

    def pair(*dims):
        return [dma(dims), dma(dims)]

    return pl.pallas_call(
        functools.partial(step_kernel, scale),
        out_shape=(
            jax.ShapeDtypeStruct((shard_rows, width), bf16),
            jax.ShapeDtypeStruct((groups * capacity, width), bf16),
        ),
        in_specs=[pl.BlockSpec(memory_space=pltpu.SMEM), far, vmem, vmem, far, far, far],
        out_specs=(vmem, vmem),
        scratch_shapes=[
            room(table.shape, bf16),
            room(w_in.shape, bf16),
            room(w_out.shape, bf16),
            room(cotangent.shape, bf16),
            dma((4,)),
            room((slots, width), bf16),
            room((1, slots), i32),
            room((1, groups * capacity), i32),
            room(block, bf16),
            room(block, bf16),
            room((groups, 1, 128), i32),
            room((groups, 1, 128), i32),
            room(block, bf16),
            room(block, bf16),
        ]
        + pair(groups)
        + pair(groups)
        + [
            room((slots, 4 * width), f32),
            room((slots, 4 * width), bf16),
            room((slots, 4 * width), bf16),
            room(block, bf16),
            room((groups // 2, capacity, width), bf16),
            room((NX, NY) + piece, bf16),
            room((NX, NY) + piece, bf16),
            room((NY,) + piece, bf16),
            room((NY,) + piece, bf16),
            room((NX, NY) + piece, bf16),
            room((NX,) + small, bf16),
            room((NX,) + small, bf16),
            room((NY,) + small, bf16),
            room((NX,) + small, bf16),
            room((groups, NX) + small, bf16),
        ]
        + pair(groups)
        + pair(groups)
        + pair(NX, NY)
        + pair(NY)
        + pair(NY)
        + pair(NX, NY)
        + pair(NX)
        + pair(NY)
        + pair(NX)
        + pair(groups)
        + pair(groups // 2)
        + [
            dma((groups,)),
            room((NY,) + piece, bf16),
            room((groups // 2, capacity, width), bf16),
            room((groups // 2, capacity, width), bf16),
        ],
        compiler_params=pltpu.CompilerParams(
            collective_id=0, has_side_effects=True, vmem_limit_bytes=60 << 20
        ),
    )(lengths, table, owners, rows, w_in, w_out, cotangent)


def per_device(table, history_shard, history_row, lengths, w_in, w_out, cotangent):
    shard_rows, model_width = table.shape
    samples_here, seq_span = history_row.shape
    groups = lax.axis_size("table")
    copies = lax.axis_size("dp")
    slot_count = samples_here * seq_span
    capacity = 2 * slot_count // groups
    total_slots = slot_count * copies * groups
    grad_scale = 1.0 / math.sqrt(total_slots)
    table_sum, dense_grad = step(
        lengths,
        table,
        history_shard.reshape(1, slot_count),
        history_row.reshape(1, slot_count),
        w_in,
        w_out,
        cotangent.reshape(slot_count, model_width),
        groups,
        capacity,
        grad_scale,
    )
    table_grad = table_sum.astype(jnp.float32)
    return (table_grad, dense_grad)


def solution(mesh):
    in_specs = (
        P("table", None),
        P(("dp", "table"), None, None),
        P(("dp", "table"), None),
        P(("dp", "table")),
        P(),
        P(),
        P(("dp", "table"), None, None),
    )
    out_specs = (P("table", None), P())
    return jax.shard_map(
        per_device, mesh=mesh, in_specs=in_specs, out_specs=out_specs, check_vma=False
    )
```

```python
import functools
import math

import jax
import jax.numpy as jnp
from jax import lax
from jax.experimental import pallas as pl
from jax.experimental.pallas import tpu as pltpu
from jax.sharding import PartitionSpec as P

HEADS = 4
NX = 4
NY = 8
MESH = pl.DeviceIdType.MESH


def send(src, dst, send_sem, recv_sem, **where):
    return pltpu.make_async_remote_copy(
        src_ref=src,
        dst_ref=dst,
        send_sem=send_sem,
        recv_sem=recv_sem,
        device_id=where,
        device_id_type=MESH,
    )


def each(start, stop, body):
    def step(i, carry):
        body(i)
        return carry

    lax.fori_loop(start, stop, step, 0)


def exchange_kernel(
    scale,
    outgoing,
    dense_part,
    incoming,
    table_out,
    dense_out,
    arrived,
    dense_arr,
    part,
    x_in,
    x_sum,
    y_in,
    whole,
    dx_out,
    dx_in,
    dy_in,
    d_row,
    d_all,
    z_s,
    z_r,
    dz_s,
    dz_r,
    x_s,
    x_r,
    y_s,
    y_r,
    gy_s,
    gy_r,
    gx_s,
    gx_r,
    dx_s,
    dx_r,
    dy_s,
    dy_r,
    dgx_s,
    dgx_r,
    dgz_s,
    dgz_r,
    ds_s,
    ds_r,
    side_s,
    x_mid,
    d_side,
    d_pair,
    d_mid,
):
    nz, cap, width = outgoing.shape
    rows = table_out.shape[0]
    x_rows = rows // NX
    half = x_rows // 2
    me = lax.axis_index("table")
    spot = lax.axis_index("dp")
    x = spot // NY
    y = lax.rem(spot, NY)
    f32, bf16 = jnp.float32, jnp.bfloat16

    def zp(k):
        return lax.rem(me + k, nz)

    def xp(k):
        return lax.rem(x + k, NX)

    def yp(k):
        return lax.rem(y + k, NY)

    side = me + 1 - 2 * lax.rem(me, 2)
    x1 = x + 1 - 2 * lax.rem(x, 2)
    x2 = lax.rem(x + 2, NX)
    x3 = NX - 1 - x

    def first(c):
        return x1 + lax.rem(c, 2) * (x3 - x1)

    def second(c):
        return x3 + lax.rem(c, 2) * (x1 - x3)

    def core(k):
        return lax.rem(me + 2 * k, nz)

    def at_x(px):
        return px * NY + y

    def at_y(py):
        return x * NY + py

    def z_copy(p):
        return send(outgoing.at[p], arrived.at[me], z_s.at[p], z_r.at[me], table=p)

    def z_wait(p):
        send(outgoing.at[p], arrived.at[p], z_s.at[p], z_r.at[p], table=p).wait_recv()

    def ds_copy(k):
        p = lax.rem(side + 2 * k, nz)
        return send(dense_part.at[p], d_side.at[k], ds_s.at[k], ds_r.at[k], table=side)

    def dz_copy(k):
        return send(d_mid.at[k], dense_arr.at[k], dz_s.at[k], dz_r.at[k], table=core(k))

    each(1, nz, lambda k: z_copy(zp(k)).start())
    each(0, nz // 2, lambda k: ds_copy(k).start())
    arrived[me] = outgoing[me]

    def pair_up(k):
        ds_copy(k).wait_recv()
        mine = dense_part[core(k)].astype(f32) + d_side[k].astype(f32)
        d_pair[k] = mine.astype(bf16)

    def dx_copy(p):
        return send(dx_out.at[p], dx_in.at[x], dx_s.at[p], dx_r.at[x], dp=at_x(p))

    def dx_wait(p):
        send(dx_out.at[p], dx_in.at[p], dx_s.at[p], dx_r.at[p], dp=at_x(p)).wait_recv()

    each(0, nz // 2, pair_up)
    for c in range(NX):
        dx_out[c] = d_pair[:, :, c * 128 : (c + 1) * 128]
    each(1, NX, lambda k: dx_copy(xp(k)).start())
    dx_in[x] = dx_out[x]
    each(1, NX, lambda k: dx_wait(xp(k)))
    d_total = dx_in[0].astype(f32)
    for k in range(1, NX):
        d_total = d_total + dx_in[k].astype(f32)
    d_mid[...] = d_total.astype(bf16)
    each(1, nz, lambda k: z_wait(zp(k)))
    each(1, nz // 2, lambda k: dz_copy(k).start())

    def xa_copy(c):
        p = first(c)
        return send(part.at[p, c], x_in.at[0, c], x_s.at[0, c], x_r.at[0, c], dp=at_x(p))

    def xb_copy(c):
        p = first(c)
        return send(part.at[x2, c], x_in.at[1, c], x_s.at[1, c], x_r.at[1, c], dp=at_x(p))

    def xc_copy(c):
        p = second(c)
        return send(x_mid.at[c], x_in.at[2, c], x_s.at[2, c], x_r.at[2, c], dp=at_x(p))

    def make_part(p):
        line = lax.broadcasted_iota(jnp.int32, (x_rows, nz * cap), 0) + p * x_rows
        pick = (line == incoming[...]).astype(f32).astype(bf16)
        got = arrived[...].reshape(nz * cap, width)
        block = jnp.dot(pick, got, preferred_element_type=f32).astype(bf16)
        for c in range(NY):
            part[p, c] = block[
                (c % 2) * half : (c % 2 + 1) * half, (c // 2) * 128 : (c // 2 + 1) * 128
            ]

    def x_start(c):
        xb_copy(c).start()
        xa_copy(c).start()

    def x_middle(c):
        xb_copy(c).wait_recv()
        held = part[second(c), c].astype(f32) + x_in[1, c].astype(f32)
        x_mid[c] = held.astype(bf16)
        xc_copy(c).start()

    make_part(x2)
    make_part(x1)
    each(0, NY // 2, lambda i: x_start(2 * lax.rem(y // 2 + 1 + i, NY // 2)))
    make_part(x3)
    each(0, NY // 2, lambda i: x_start(2 * lax.rem(y // 2 + 1 + i, NY // 2) + 1))
    make_part(x)
    each(0, NY // 2, lambda i: x_middle(2 * lax.rem(y // 2 + 1 + i, NY // 2)))
    each(0, NY // 2, lambda i: x_middle(2 * lax.rem(y // 2 + 1 + i, NY // 2) + 1))

    def y_copy(c):
        return send(x_sum.at[c], y_in.at[y], y_s.at[c], y_r.at[y], dp=at_y(c))

    def y_wait(c):
        send(x_sum.at[c], y_in.at[c], y_s.at[c], y_r.at[c], dp=at_y(c)).wait_recv()

    def sum_x(c):
        xa_copy(c).wait_recv()
        xc_copy(c).wait_recv()
        total = part[x, c].astype(f32) + x_in[0, c].astype(f32) + x_in[2, c].astype(f32)
        x_sum[c] = total.astype(bf16)

    def y_stage(j):
        c = yp(j)
        sum_x(c)
        y_copy(c).start()

    each(1, NY, y_stage)
    sum_x(y)

    def dy_copy(p):
        return send(dy_in.at[y], dy_in.at[y], dy_s.at[p], dy_r.at[y], dp=at_y(p))

    def dy_wait(p):
        send(dy_in.at[p], dy_in.at[p], dy_s.at[p], dy_r.at[p], dp=at_y(p)).wait_recv()

    each(1, nz // 2, lambda k: dz_copy(k).wait_recv())
    d_total = d_mid[0].astype(f32)
    for k in range(1, nz // 2):
        d_total = d_total + dense_arr[k].astype(f32)
    dy_in[y] = d_total.astype(bf16)
    each(1, NY, lambda k: dy_copy(yp(k)).start())

    total = x_sum[y].astype(f32)
    for j in range(1, NY):
        c = yp(j)
        y_wait(c)
        total = total + y_in[c].astype(f32)
    whole[x, y] = total.astype(bf16)

    def gy_copy(p):
        return send(whole.at[x, y], whole.at[x, y], gy_s.at[p], gy_r.at[y], dp=at_y(p))

    def gy_wait(p):
        send(whole.at[x, p], whole.at[x, p], gy_s.at[p], gy_r.at[p], dp=at_y(p)).wait_recv()

    def gx_copy(p, c):
        return send(whole.at[x, c], whole.at[x, c], gx_s.at[p, c], gx_r.at[x, c], dp=at_x(p))

    def gx_wait(p, c):
        send(whole.at[p, c], whole.at[p, c], gx_s.at[p, c], gx_r.at[p, c], dp=at_x(p)).wait_recv()

    def gf_copy(c):
        q = second(c)
        p = first(c)
        return send(whole.at[q, c], whole.at[q, c], gx_s.at[x2, c], gx_r.at[q, c], dp=at_x(p))

    def gx_both(c):
        gx_copy(second(c), c).start()
        gx_copy(first(c), c).start()

    each(1, NY, lambda k: gy_copy(yp(k)).start())
    gx_both(y)

    def pass_on(j):
        c = yp(j)
        gy_wait(c)
        gx_both(c)

    each(1, NY // 2, pass_on)

    def dgx_copy(p):
        return send(d_row.at[x], d_row.at[x], dgx_s.at[p], dgx_r.at[x], dp=at_x(p))

    def dgx_wait(p):
        send(d_row.at[p], d_row.at[p], dgx_s.at[p], dgx_r.at[p], dp=at_x(p)).wait_recv()

    each(1, NY, lambda k: dy_wait(yp(k)))
    d_total = dy_in[0].astype(f32)
    for k in range(1, NY):
        d_total = d_total + dy_in[k].astype(f32)
    d_row[x] = (d_total * scale).astype(bf16)
    each(1, NX, lambda k: dgx_copy(xp(k)).start())
    each(NY // 2, NY, pass_on)

    def dgz_copy(p):
        return send(d_all.at[me], d_all.at[me], dgz_s.at[p], dgz_r.at[me], table=p)

    def dgz_wait(p):
        send(d_all.at[p], d_all.at[p], dgz_s.at[p], dgz_r.at[p], table=p).wait_recv()

    def side_copy(p):
        return send(d_all.at[p], d_all.at[p], side_s.at[p], dgz_r.at[p], table=side)

    each(1, NX, lambda k: dgx_wait(xp(k)))
    d_all[me] = d_row[...]
    each(1, nz // 2, lambda k: dgz_copy(core(k)).start())
    side_copy(me).start()

    def forward(j):
        c = yp(j)
        gx_wait(second(c), c)
        gf_copy(c).start()

    each(0, NY, forward)

    def gather_side(k):
        p = core(k)
        dgz_wait(p)
        side_copy(p).start()

    each(1, nz // 2, gather_side)

    def gx_rest(c):
        gx_wait(first(c), c)
        gx_wait(x2, c)

    each(0, NY, gx_rest)
    for px in range(NX):
        for c in range(NY):
            table_out[
                px * x_rows + (c % 2) * half : px * x_rows + (c % 2 + 1) * half,
                (c // 2) * 128 : (c // 2 + 1) * 128,
            ] = whole[px, c]
    each(0, nz // 2, lambda k: dgz_wait(lax.rem(side + 2 * k, nz)))
    for t in range(nz):
        for c in range(NX):
            dense_out[t * cap : (t + 1) * cap, c * 128 : (c + 1) * 128] = d_all[t, c]

    def sent_side(k):
        ds_copy(k).wait_send()
        side_copy(core(k)).wait_send()

    def sent_core(k):
        dz_copy(k).wait_send()
        dgz_copy(core(k)).wait_send()

    def sent_x(k):
        p = xp(k)
        dx_copy(p).wait_send()
        dgx_copy(p).wait_send()

    def sent_piece(c):
        xa_copy(c).wait_send()
        xb_copy(c).wait_send()
        xc_copy(c).wait_send()
        gx_copy(first(c), c).wait_send()
        gx_copy(second(c), c).wait_send()
        gf_copy(c).wait_send()

    def sent_y(k):
        p = yp(k)
        y_copy(p).wait_send()
        gy_copy(p).wait_send()
        dy_copy(p).wait_send()

    each(1, nz, lambda k: z_copy(zp(k)).wait_send())
    each(0, nz // 2, sent_side)
    each(1, nz // 2, sent_core)
    each(0, NY, sent_piece)
    each(1, NX, sent_x)
    each(1, NY, sent_y)


def dot_first(a, b):
    return lax.dot_general(a, b, (((0,), (0,)), ((), ())), preferred_element_type=jnp.float32)


def hot(shape, index):
    line = lax.broadcasted_iota(jnp.int32, shape, 0)
    return (line == index).astype(jnp.float32).astype(jnp.bfloat16)


def fetch_kernel(
    ready,
    table_here,
    table,
    owners,
    rows,
    embedded,
    position,
    incoming,
    req_out,
    req_in,
    reply,
    got,
    q_s,
    q_r,
    r_s,
    r_r,
):
    nz, cap, width = got.shape
    slots = owners.shape[1]
    shard_rows = table.shape[0]
    per = 128 // cap
    me = lax.axis_index("table")
    f32, bf16 = jnp.float32, jnp.bfloat16

    def zp(k):
        return lax.rem(me + k, nz)

    own = owners[...]
    hits = (lax.broadcasted_iota(jnp.int32, (nz, slots), 0) == own).astype(f32)
    earlier = (
        lax.broadcasted_iota(jnp.int32, (slots, slots), 0)
        < lax.broadcasted_iota(jnp.int32, (slots, slots), 1)
    ).astype(f32)
    ahead = jnp.dot(hits.astype(bf16), earlier.astype(bf16), preferred_element_type=f32)
    rank = jnp.sum(hits * ahead, axis=0, keepdims=True).astype(jnp.int32)
    place = own * cap + rank
    position[...] = place
    pick = hot((nz * 128, slots), own * 128 + lax.rem(me, per) * cap + rank)
    wanted = rows[...]
    high = lax.shift_right_logical(wanted, 8)
    low = wanted & 255
    which = lax.broadcasted_iota(jnp.int32, (8, slots), 0)
    both = jnp.where(which == 0, high, jnp.where(which == 1, low, 0)).astype(f32).astype(bf16)
    found = lax.dot_general(both, pick, (((1,), (1,)), ((), ())), preferred_element_type=f32)
    asked = (found[0:1] * 256.0 + found[1:2]).astype(jnp.int32)
    for p in range(nz):
        req_out[p] = asked[:, p * 128 : (p + 1) * 128]
    ready()

    def q_copy(p):
        return send(req_out.at[p], req_in.at[me], q_s.at[p], q_r.at[me], table=p)

    def q_wait(p):
        send(req_out.at[p], req_in.at[p], q_s.at[p], q_r.at[p], table=p).wait_recv()

    def r_copy(p):
        return send(reply.at[p], got.at[me], r_s.at[p], r_r.at[me], table=p)

    def r_wait(p):
        send(reply.at[p], got.at[p], r_s.at[p], r_r.at[p], table=p).wait_recv()

    each(1, nz, lambda k: q_copy(zp(k)).start())
    req_in[me] = req_out[me]
    each(1, nz, lambda k: q_wait(zp(k)))
    table_here()
    for g in range(nz // per):
        line = req_in[g * per]
        for j in range(1, per):
            line = line + req_in[g * per + j]
        incoming[:, g * 128 : (g + 1) * 128] = line
        block = dot_first(hot((shard_rows, 128), line), table[...]).astype(bf16)
        for j in range(per):
            reply[g * per + j] = block[j * cap : (j + 1) * cap]
    each(1, nz, lambda k: r_copy(zp(k)).start())
    got[me] = reply[me]
    each(1, nz, lambda k: r_wait(zp(k)))
    spread = hot((nz * cap, slots), place)
    embedded[...] = dot_first(spread, got[...].reshape(nz * cap, width)).astype(bf16)

    def sent(k):
        q_copy(zp(k)).wait_send()
        r_copy(zp(k)).wait_send()

    each(1, nz, sent)


def centre(values):
    shifted = values - jnp.mean(values, axis=-1, keepdims=True)
    spread = lax.rsqrt(jnp.mean(shifted * shifted, axis=-1, keepdims=True) + 1e-06)
    return shifted * spread, spread


def centre_back(grad, unit, spread):
    along = jnp.mean(grad * unit, axis=-1, keepdims=True)
    return spread * (grad - jnp.mean(grad, axis=-1, keepdims=True) - unit * along)


def dot_last(a, b):
    return lax.dot_general(a, b, (((1,), (1,)), ((), ())), preferred_element_type=jnp.float32)


def dot_plain(a, b):
    return jnp.dot(a, b, preferred_element_type=jnp.float32)


def layer_kernel(
    lengths, embedded, position, w_in, w_out, cotangent, outgoing, dense_part, before, after, grad
):
    f32, bf16 = jnp.float32, jnp.bfloat16
    span, width = embedded.shape
    head = width // HEADS
    length = lengths[0]
    share = 1.0 / length.astype(f32)
    unit, spread = centre(embedded[...].astype(f32))
    normed = unit.astype(bf16)
    for b in range(4):
        cols = slice(b * width, (b + 1) * width)
        made = dot_plain(normed, w_in[:, cols])
        before[:, cols] = made
        if b > 0:
            after[:, cols] = (made * jax.nn.sigmoid(made)).astype(bf16)
    row = lax.broadcasted_iota(jnp.int32, (span, span), 0)
    col = lax.broadcasted_iota(jnp.int32, (span, span), 1)
    live = (col <= row) & (col < length)
    scale = head ** (-0.5)

    def columns(part, h):
        return slice(part * width + h * head, part * width + (h + 1) * head)

    attended = []
    kept = []
    for h in range(HEADS):
        scores = dot_last(after[:, columns(2, h)], after[:, columns(3, h)]) * scale
        gain = jax.nn.sigmoid(scores)
        weights = (jnp.where(live, scores * gain, 0.0) * share).astype(bf16)
        slope = jnp.where(live, gain * (1.0 + scores * (1.0 - gain)), 0.0) * share
        attended.append(dot_plain(weights, after[:, columns(1, h)]))
        kept.append((weights, slope))
    mid, mid_spread = centre(jnp.concatenate(attended, axis=1))
    gate_in = before[:, :width]
    gate_sig = jax.nn.sigmoid(gate_in)
    gate = gate_in * gate_sig
    mixed = (mid * gate).astype(bf16)
    item = lax.broadcasted_iota(jnp.int32, (span, width), 0)
    seed = jnp.where(item < length, cotangent[...].astype(f32), 0.0)
    seed_low = seed.astype(bf16)
    dense_part[...] = dot_first(mixed, seed_low).astype(bf16).reshape(dense_part.shape)

    d_mixed = dot_last(seed_low, w_out[...]).astype(bf16).astype(f32)
    grad[:, :width] = (d_mixed * mid * (gate_sig * (1.0 + gate_in * (1.0 - gate_sig)))).astype(bf16)
    d_att = centre_back(d_mixed * gate, mid, mid_spread).astype(bf16)

    def keep(part, h, value):
        cols = columns(part, h)
        x = before[:, cols]
        sig = jax.nn.sigmoid(x)
        grad[:, cols] = (value * (sig * (1.0 + x * (1.0 - sig)))).astype(bf16)

    for h in range(HEADS):
        weights, slope = kept[h]
        d_head = d_att[:, h * head : (h + 1) * head]
        d_scores = (dot_last(d_head, after[:, columns(1, h)]) * slope * scale).astype(bf16)
        keep(1, h, dot_first(weights, d_head))
        keep(2, h, dot_plain(d_scores, after[:, columns(3, h)]))
        keep(3, h, dot_first(d_scores, after[:, columns(2, h)]))
    d_normed = dot_last(grad[:, :width], w_in[:, :width])
    for b in range(1, 4):
        cols = slice(b * width, (b + 1) * width)
        d_normed = d_normed + dot_last(grad[:, cols], w_in[:, cols])
    row_grad = (centre_back(d_normed, unit, spread) + seed).astype(bf16)
    nz, cap, _ = outgoing.shape
    spots = hot((nz * cap, span), position[...])
    outgoing[...] = dot_plain(spots, row_grad).astype(bf16).reshape(outgoing.shape)


def step_kernel(
    scale,
    lengths,
    table_far,
    owners,
    rows,
    w_in_far,
    w_out_far,
    cotangent_far,
    table_out,
    dense_out,
    table,
    w_in,
    w_out,
    cotangent,
    near_s,
    embedded,
    position,
    incoming,
    outgoing,
    dense_part,
    *scratch,
):
    nz = outgoing.shape[0]
    me = lax.axis_index("table")
    spot = lax.axis_index("dp")
    x = spot // NY
    y = lax.rem(spot, NY)
    barrier = pltpu.get_barrier_semaphore()

    def greet(axis, peer):
        pl.semaphore_signal(barrier, inc=1, device_id={axis: peer}, device_id_type=MESH)

    each(1, nz, lambda k: greet("table", lax.rem(me + k, nz)))
    each(1, NX, lambda k: greet("dp", lax.rem(x + k, NX) * NY + y))
    each(1, NY, lambda k: greet("dp", x * NY + lax.rem(y + k, NY)))

    pairs = ((table_far, table), (w_in_far, w_in), (w_out_far, w_out), (cotangent_far, cotangent))
    copies = [pltpu.make_async_copy(a, b, near_s.at[i]) for i, (a, b) in enumerate(pairs)]
    for copy in copies:
        copy.start()

    def ready():
        pl.semaphore_wait(barrier, nz - 1 + NX - 1 + NY - 1)

    fetch_kernel(
        ready, copies[0].wait, table, owners, rows, embedded, position, incoming, *scratch[:8]
    )
    for copy in copies[1:]:
        copy.wait()
    layer_kernel(
        lengths,
        embedded,
        position,
        w_in,
        w_out,
        cotangent,
        outgoing,
        dense_part,
        *scratch[8:11],
    )
    exchange_kernel(
        scale, outgoing, dense_part, incoming, table_out, dense_out, *scratch[11:]
    )


def step(lengths, table, owners, rows, w_in, w_out, cotangent, groups, capacity, scale):
    shard_rows, width = table.shape
    slots = owners.shape[1]
    bf16, f32, i32 = jnp.bfloat16, jnp.float32, jnp.int32
    piece = (shard_rows // NX // 2, 128)
    small = (capacity, 128)
    block = (groups, capacity, width)
    vmem = pl.BlockSpec(memory_space=pltpu.VMEM)
    far = pl.BlockSpec(memory_space=pl.ANY)
    dma = pltpu.SemaphoreType.DMA
    room = pltpu.VMEM

    def pair(*dims):
        return [dma(dims), dma(dims)]

    return pl.pallas_call(
        functools.partial(step_kernel, scale),
        out_shape=(
            jax.ShapeDtypeStruct((shard_rows, width), bf16),
            jax.ShapeDtypeStruct((groups * capacity, width), bf16),
        ),
        in_specs=[pl.BlockSpec(memory_space=pltpu.SMEM), far, vmem, vmem, far, far, far],
        out_specs=(vmem, vmem),
        scratch_shapes=[
            room(table.shape, bf16),
            room(w_in.shape, bf16),
            room(w_out.shape, bf16),
            room(cotangent.shape, bf16),
            dma((4,)),
            room((slots, width), bf16),
            room((1, slots), i32),
            room((1, groups * capacity), i32),
            room(block, bf16),
            room(block, bf16),
            room((groups, 1, 128), i32),
            room((groups, 1, 128), i32),
            room(block, bf16),
            room(block, bf16),
        ]
        + pair(groups)
        + pair(groups)
        + [
            room((slots, 4 * width), f32),
            room((slots, 4 * width), bf16),
            room((slots, 4 * width), bf16),
            room(block, bf16),
            room((groups // 2,) + small, bf16),
            room((NX, NY) + piece, bf16),
            room((NX, NY) + piece, bf16),
            room((NY,) + piece, bf16),
            room((NY,) + piece, bf16),
            room((NX, NY) + piece, bf16),
            room((NX, groups // 2) + small, bf16),
            room((NX, groups // 2) + small, bf16),
            room((NY,) + small, bf16),
            room((NX,) + small, bf16),
            room((groups, NX) + small, bf16),
        ]
        + pair(groups)
        + pair(groups)
        + pair(NX, NY)
        + pair(NY)
        + pair(NY)
        + pair(NX, NY)
        + pair(NX)
        + pair(NY)
        + pair(NX)
        + pair(groups)
        + pair(groups // 2)
        + [
            dma((groups,)),
            room((NY,) + piece, bf16),
            room((groups // 2, capacity, width), bf16),
            room((groups // 2, capacity, width), bf16),
            room((groups // 2,) + small, bf16),
        ],
        compiler_params=pltpu.CompilerParams(
            collective_id=0, has_side_effects=True, vmem_limit_bytes=60 << 20
        ),
    )(lengths, table, owners, rows, w_in, w_out, cotangent)


def per_device(table, history_shard, history_row, lengths, w_in, w_out, cotangent):
    shard_rows, model_width = table.shape
    samples_here, seq_span = history_row.shape
    groups = lax.axis_size("table")
    copies = lax.axis_size("dp")
    slot_count = samples_here * seq_span
    capacity = 2 * slot_count // groups
    total_slots = slot_count * copies * groups
    grad_scale = 1.0 / math.sqrt(total_slots)
    table_sum, dense_grad = step(
        lengths,
        table,
        history_shard.reshape(1, slot_count),
        history_row.reshape(1, slot_count),
        w_in,
        w_out,
        cotangent.reshape(slot_count, model_width),
        groups,
        capacity,
        grad_scale,
    )
    table_grad = table_sum.astype(jnp.float32)
    return (table_grad, dense_grad)


def solution(mesh):
    in_specs = (
        P("table", None),
        P(("dp", "table"), None, None),
        P(("dp", "table"), None),
        P(("dp", "table")),
        P(),
        P(),
        P(("dp", "table"), None, None),
    )
    out_specs = (P("table", None), P())
    return jax.shard_map(
        per_device, mesh=mesh, in_specs=in_specs, out_specs=out_specs, check_vma=False
    )
```

```python
import functools
import math

import jax
import jax.numpy as jnp
from jax import lax
from jax.experimental import pallas as pl
from jax.experimental.pallas import tpu as pltpu
from jax.sharding import PartitionSpec as P

HEADS = 4
NX = 4
NY = 8
MESH = pl.DeviceIdType.MESH


def send(src, dst, send_sem, recv_sem, **where):
    return pltpu.make_async_remote_copy(
        src_ref=src,
        dst_ref=dst,
        send_sem=send_sem,
        recv_sem=recv_sem,
        device_id=where,
        device_id_type=MESH,
    )


def each(start, stop, body):
    def step(i, carry):
        body(i)
        return carry

    lax.fori_loop(start, stop, step, 0)


def exchange_kernel(
    scale,
    outgoing,
    dense_part,
    incoming,
    table_out,
    dense_out,
    arrived,
    dense_arr,
    part,
    x_in,
    x_sum,
    y_in,
    whole,
    dx_out,
    dx_in,
    dy_in,
    d_row,
    d_all,
    z_s,
    z_r,
    dz_s,
    dz_r,
    x_s,
    x_r,
    y_s,
    y_r,
    gy_s,
    gy_r,
    gx_s,
    gx_r,
    dx_s,
    dx_r,
    dy_s,
    dy_r,
    dgx_s,
    dgx_r,
    dgz_s,
    dgz_r,
    ds_s,
    ds_r,
    side_s,
    x_mid,
    d_side,
    d_pair,
    d_mid,
):
    nz, cap, width = outgoing.shape
    rows = table_out.shape[0]
    x_rows = rows // NX
    half = x_rows // 2
    me = lax.axis_index("table")
    spot = lax.axis_index("dp")
    x = spot // NY
    y = lax.rem(spot, NY)
    f32, bf16 = jnp.float32, jnp.bfloat16

    def zp(k):
        return lax.rem(me + nz // 2 + (k // 2) * (1 - 2 * lax.rem(k, 2)) + nz, nz)

    def xp(k):
        return lax.rem(x + k, NX)

    def yp(k):
        return lax.rem(y + k, NY)

    side = me + 1 - 2 * lax.rem(me, 2)
    x1 = x + 1 - 2 * lax.rem(x, 2)
    x2 = lax.rem(x + 2, NX)
    x3 = NX - 1 - x

    def first(c):
        return x1 + lax.rem(c, 2) * (x3 - x1)

    def second(c):
        return x3 + lax.rem(c, 2) * (x1 - x3)

    def core(k):
        return lax.rem(me + 2 * k, nz)

    def at_x(px):
        return px * NY + y

    def at_y(py):
        return x * NY + py

    def z_copy(p):
        return send(outgoing.at[p], arrived.at[me], z_s.at[p], z_r.at[me], table=p)

    def z_wait(p):
        send(outgoing.at[p], arrived.at[p], z_s.at[p], z_r.at[p], table=p).wait_recv()

    def ds_copy(k):
        p = lax.rem(side + 2 * k, nz)
        return send(dense_part.at[p], d_side.at[k], ds_s.at[k], ds_r.at[k], table=side)

    def dz_copy(k):
        return send(d_mid.at[k], dense_arr.at[k], dz_s.at[k], dz_r.at[k], table=core(k))

    each(1, nz, lambda k: z_copy(zp(k)).start())
    each(0, nz // 2, lambda k: ds_copy(k).start())
    arrived[me] = outgoing[me]

    def pair_up(k):
        ds_copy(k).wait_recv()
        mine = dense_part[core(k)].astype(f32) + d_side[k].astype(f32)
        d_pair[k] = mine.astype(bf16)

    def dx_copy(p):
        return send(dx_out.at[p], dx_in.at[x], dx_s.at[p], dx_r.at[x], dp=at_x(p))

    def dx_wait(p):
        send(dx_out.at[p], dx_in.at[p], dx_s.at[p], dx_r.at[p], dp=at_x(p)).wait_recv()

    each(0, nz // 2, pair_up)
    for c in range(NX):
        dx_out[c] = d_pair[:, :, c * 128 : (c + 1) * 128]
    each(1, NX, lambda k: dx_copy(xp(k)).start())
    dx_in[x] = dx_out[x]
    each(1, NX, lambda k: dx_wait(xp(k)))
    d_total = dx_in[0].astype(f32)
    for k in range(1, NX):
        d_total = d_total + dx_in[k].astype(f32)
    d_mid[...] = d_total.astype(bf16)
    each(1, nz, lambda k: z_wait(zp(k)))
    each(1, nz // 2, lambda k: dz_copy(k).start())

    def xa_copy(c):
        p = first(c)
        return send(part.at[p, c], x_in.at[0, c], x_s.at[0, c], x_r.at[0, c], dp=at_x(p))

    def xb_copy(c):
        p = first(c)
        return send(part.at[x2, c], x_in.at[1, c], x_s.at[1, c], x_r.at[1, c], dp=at_x(p))

    def xc_copy(c):
        p = second(c)
        return send(x_mid.at[c], x_in.at[2, c], x_s.at[2, c], x_r.at[2, c], dp=at_x(p))

    def make_part(p):
        line = lax.broadcasted_iota(jnp.int32, (x_rows, nz * cap), 0) + p * x_rows
        pick = (line == incoming[...]).astype(f32).astype(bf16)
        got = arrived[...].reshape(nz * cap, width)
        block = jnp.dot(pick, got, preferred_element_type=f32).astype(bf16)
        for c in range(NY):
            part[p, c] = block[
                (c % 2) * half : (c % 2 + 1) * half, (c // 2) * 128 : (c // 2 + 1) * 128
            ]

    def x_start(c):
        xb_copy(c).start()
        xa_copy(c).start()

    def x_middle(c):
        xb_copy(c).wait_recv()
        held = part[second(c), c].astype(f32) + x_in[1, c].astype(f32)
        x_mid[c] = held.astype(bf16)
        xc_copy(c).start()

    make_part(x2)
    make_part(x1)
    each(0, NY // 2, lambda i: x_start(2 * lax.rem(y // 2 + 1 + i, NY // 2)))
    make_part(x3)
    each(0, NY // 2, lambda i: x_start(2 * lax.rem(y // 2 + 1 + i, NY // 2) + 1))
    make_part(x)
    each(0, NY // 2, lambda i: x_middle(2 * lax.rem(y // 2 + 1 + i, NY // 2)))
    each(0, NY // 2, lambda i: x_middle(2 * lax.rem(y // 2 + 1 + i, NY // 2) + 1))

    def y_copy(c):
        return send(x_sum.at[c], y_in.at[y], y_s.at[c], y_r.at[y], dp=at_y(c))

    def y_wait(c):
        send(x_sum.at[c], y_in.at[c], y_s.at[c], y_r.at[c], dp=at_y(c)).wait_recv()

    def sum_x(c):
        xa_copy(c).wait_recv()
        xc_copy(c).wait_recv()
        total = part[x, c].astype(f32) + x_in[0, c].astype(f32) + x_in[2, c].astype(f32)
        x_sum[c] = total.astype(bf16)

    def y_stage(j):
        c = yp(j)
        sum_x(c)
        y_copy(c).start()

    each(1, NY, y_stage)
    sum_x(y)

    def dy_copy(p):
        return send(dy_in.at[y], dy_in.at[y], dy_s.at[p], dy_r.at[y], dp=at_y(p))

    def dy_wait(p):
        send(dy_in.at[p], dy_in.at[p], dy_s.at[p], dy_r.at[p], dp=at_y(p)).wait_recv()

    each(1, nz // 2, lambda k: dz_copy(k).wait_recv())
    d_total = d_mid[0].astype(f32)
    for k in range(1, nz // 2):
        d_total = d_total + dense_arr[k].astype(f32)
    dy_in[y] = d_total.astype(bf16)
    each(1, NY, lambda k: dy_copy(yp(k)).start())

    total = x_sum[y].astype(f32)
    for j in range(1, NY):
        c = yp(j)
        y_wait(c)
        total = total + y_in[c].astype(f32)
    whole[x, y] = total.astype(bf16)

    def gy_copy(p):
        return send(whole.at[x, y], whole.at[x, y], gy_s.at[p], gy_r.at[y], dp=at_y(p))

    def gy_wait(p):
        send(whole.at[x, p], whole.at[x, p], gy_s.at[p], gy_r.at[p], dp=at_y(p)).wait_recv()

    def gx_copy(p, c):
        return send(whole.at[x, c], whole.at[x, c], gx_s.at[p, c], gx_r.at[x, c], dp=at_x(p))

    def gx_wait(p, c):
        send(whole.at[p, c], whole.at[p, c], gx_s.at[p, c], gx_r.at[p, c], dp=at_x(p)).wait_recv()

    def gf_copy(c):
        q = second(c)
        p = first(c)
        return send(whole.at[q, c], whole.at[q, c], gx_s.at[x2, c], gx_r.at[q, c], dp=at_x(p))

    def gx_both(c):
        gx_copy(second(c), c).start()
        gx_copy(first(c), c).start()

    each(1, NY, lambda k: gy_copy(yp(k)).start())
    gx_both(y)

    def pass_on(j):
        c = yp(j)
        gy_wait(c)
        gx_both(c)

    each(1, NY // 2, pass_on)

    def dgx_copy(p):
        return send(d_row.at[x], d_row.at[x], dgx_s.at[p], dgx_r.at[x], dp=at_x(p))

    def dgx_wait(p):
        send(d_row.at[p], d_row.at[p], dgx_s.at[p], dgx_r.at[p], dp=at_x(p)).wait_recv()

    each(1, NY, lambda k: dy_wait(yp(k)))
    d_total = dy_in[0].astype(f32)
    for k in range(1, NY):
        d_total = d_total + dy_in[k].astype(f32)
    d_row[x] = (d_total * scale).astype(bf16)
    each(1, NX, lambda k: dgx_copy(xp(k)).start())
    each(NY // 2, NY, pass_on)

    def dgz_copy(p):
        return send(d_all.at[me], d_all.at[me], dgz_s.at[p], dgz_r.at[me], table=p)

    def dgz_wait(p):
        send(d_all.at[p], d_all.at[p], dgz_s.at[p], dgz_r.at[p], table=p).wait_recv()

    def side_copy(p):
        return send(d_all.at[p], d_all.at[p], side_s.at[p], dgz_r.at[p], table=side)

    each(1, NX, lambda k: dgx_wait(xp(k)))
    d_all[me] = d_row[...]
    each(1, nz // 2, lambda k: dgz_copy(core(k)).start())
    side_copy(me).start()

    def forward(j):
        c = yp(j)
        gx_wait(second(c), c)
        gf_copy(c).start()

    each(0, NY, forward)

    def gather_side(k):
        p = core(k)
        dgz_wait(p)
        side_copy(p).start()

    each(1, nz // 2, gather_side)

    def gx_rest(c):
        gx_wait(first(c), c)
        gx_wait(x2, c)

    each(0, NY, gx_rest)
    for px in range(NX):
        for c in range(NY):
            table_out[
                px * x_rows + (c % 2) * half : px * x_rows + (c % 2 + 1) * half,
                (c // 2) * 128 : (c // 2 + 1) * 128,
            ] = whole[px, c]
    each(0, nz // 2, lambda k: dgz_wait(lax.rem(side + 2 * k, nz)))
    for t in range(nz):
        for c in range(NX):
            dense_out[t * cap : (t + 1) * cap, c * 128 : (c + 1) * 128] = d_all[t, c]

    def sent_side(k):
        ds_copy(k).wait_send()
        side_copy(core(k)).wait_send()

    def sent_core(k):
        dz_copy(k).wait_send()
        dgz_copy(core(k)).wait_send()

    def sent_x(k):
        p = xp(k)
        dx_copy(p).wait_send()
        dgx_copy(p).wait_send()

    def sent_piece(c):
        xa_copy(c).wait_send()
        xb_copy(c).wait_send()
        xc_copy(c).wait_send()
        gx_copy(first(c), c).wait_send()
        gx_copy(second(c), c).wait_send()
        gf_copy(c).wait_send()

    def sent_y(k):
        p = yp(k)
        y_copy(p).wait_send()
        gy_copy(p).wait_send()
        dy_copy(p).wait_send()

    each(1, nz, lambda k: z_copy(zp(k)).wait_send())
    each(0, nz // 2, sent_side)
    each(1, nz // 2, sent_core)
    each(0, NY, sent_piece)
    each(1, NX, sent_x)
    each(1, NY, sent_y)


def dot_first(a, b):
    return lax.dot_general(a, b, (((0,), (0,)), ((), ())), preferred_element_type=jnp.float32)


def hot(shape, index):
    line = lax.broadcasted_iota(jnp.int32, shape, 0)
    return (line == index).astype(jnp.float32).astype(jnp.bfloat16)


def fetch_kernel(
    ready,
    table_here,
    table,
    owners,
    rows,
    embedded,
    position,
    incoming,
    req_out,
    req_in,
    reply,
    got,
    q_s,
    q_r,
    r_s,
    r_r,
):
    nz, cap, width = got.shape
    slots = owners.shape[1]
    shard_rows = table.shape[0]
    per = 128 // cap
    me = lax.axis_index("table")
    f32, bf16 = jnp.float32, jnp.bfloat16

    def zp(k):
        return lax.rem(me + nz // 2 + (k // 2) * (1 - 2 * lax.rem(k, 2)) + nz, nz)

    own = owners[...]
    hits = (lax.broadcasted_iota(jnp.int32, (nz, slots), 0) == own).astype(f32)
    earlier = (
        lax.broadcasted_iota(jnp.int32, (slots, slots), 0)
        < lax.broadcasted_iota(jnp.int32, (slots, slots), 1)
    ).astype(f32)
    ahead = jnp.dot(hits.astype(bf16), earlier.astype(bf16), preferred_element_type=f32)
    rank = jnp.sum(hits * ahead, axis=0, keepdims=True).astype(jnp.int32)
    place = own * cap + rank
    position[...] = place
    pick = hot((nz * 128, slots), own * 128 + lax.rem(me, per) * cap + rank)
    wanted = rows[...]
    high = lax.shift_right_logical(wanted, 8)
    low = wanted & 255
    which = lax.broadcasted_iota(jnp.int32, (8, slots), 0)
    both = jnp.where(which == 0, high, jnp.where(which == 1, low, 0)).astype(f32).astype(bf16)
    found = lax.dot_general(both, pick, (((1,), (1,)), ((), ())), preferred_element_type=f32)
    asked = (found[0:1] * 256.0 + found[1:2]).astype(jnp.int32)
    for p in range(nz):
        req_out[p] = asked[:, p * 128 : (p + 1) * 128]
    ready()

    def q_copy(p):
        return send(req_out.at[p], req_in.at[me], q_s.at[p], q_r.at[me], table=p)

    def q_wait(p):
        send(req_out.at[p], req_in.at[p], q_s.at[p], q_r.at[p], table=p).wait_recv()

    def r_copy(p):
        return send(reply.at[p], got.at[me], r_s.at[p], r_r.at[me], table=p)

    def r_wait(p):
        send(reply.at[p], got.at[p], r_s.at[p], r_r.at[p], table=p).wait_recv()

    each(1, nz, lambda k: q_copy(zp(k)).start())
    req_in[me] = req_out[me]
    each(1, nz, lambda k: q_wait(zp(k)))
    table_here()
    for g in range(nz // per):
        line = req_in[g * per]
        for j in range(1, per):
            line = line + req_in[g * per + j]
        incoming[:, g * 128 : (g + 1) * 128] = line
        block = dot_first(hot((shard_rows, 128), line), table[...]).astype(bf16)
        for j in range(per):
            reply[g * per + j] = block[j * cap : (j + 1) * cap]
    each(1, nz, lambda k: r_copy(zp(k)).start())
    got[me] = reply[me]
    each(1, nz, lambda k: r_wait(zp(k)))
    spread = hot((nz * cap, slots), place)
    embedded[...] = dot_first(spread, got[...].reshape(nz * cap, width)).astype(bf16)

    def sent(k):
        q_copy(zp(k)).wait_send()
        r_copy(zp(k)).wait_send()

    each(1, nz, sent)


def centre(values):
    shifted = values - jnp.mean(values, axis=-1, keepdims=True)
    spread = lax.rsqrt(jnp.mean(shifted * shifted, axis=-1, keepdims=True) + 1e-06)
    return shifted * spread, spread


def centre_back(grad, unit, spread):
    along = jnp.mean(grad * unit, axis=-1, keepdims=True)
    return spread * (grad - jnp.mean(grad, axis=-1, keepdims=True) - unit * along)


def dot_last(a, b):
    return lax.dot_general(a, b, (((1,), (1,)), ((), ())), preferred_element_type=jnp.float32)


def dot_plain(a, b):
    return jnp.dot(a, b, preferred_element_type=jnp.float32)


def layer_kernel(
    lengths, embedded, position, w_in, w_out, cotangent, outgoing, dense_part, before, after, grad
):
    f32, bf16 = jnp.float32, jnp.bfloat16
    span, width = embedded.shape
    head = width // HEADS
    length = lengths[0]
    share = 1.0 / length.astype(f32)
    unit, spread = centre(embedded[...].astype(f32))
    normed = unit.astype(bf16)
    for b in range(4):
        cols = slice(b * width, (b + 1) * width)
        made = dot_plain(normed, w_in[:, cols])
        before[:, cols] = made
        if b > 0:
            after[:, cols] = (made * jax.nn.sigmoid(made)).astype(bf16)
    row = lax.broadcasted_iota(jnp.int32, (span, span), 0)
    col = lax.broadcasted_iota(jnp.int32, (span, span), 1)
    live = (col <= row) & (col < length)
    scale = head ** (-0.5)

    def columns(part, h):
        return slice(part * width + h * head, part * width + (h + 1) * head)

    attended = []
    kept = []
    for h in range(HEADS):
        scores = dot_last(after[:, columns(2, h)], after[:, columns(3, h)]) * scale
        gain = jax.nn.sigmoid(scores)
        weights = (jnp.where(live, scores * gain, 0.0) * share).astype(bf16)
        slope = jnp.where(live, gain * (1.0 + scores * (1.0 - gain)), 0.0) * share
        attended.append(dot_plain(weights, after[:, columns(1, h)]))
        kept.append((weights, slope))
    mid, mid_spread = centre(jnp.concatenate(attended, axis=1))
    gate_in = before[:, :width]
    gate_sig = jax.nn.sigmoid(gate_in)
    gate = gate_in * gate_sig
    mixed = (mid * gate).astype(bf16)
    item = lax.broadcasted_iota(jnp.int32, (span, width), 0)
    seed = jnp.where(item < length, cotangent[...].astype(f32), 0.0)
    seed_low = seed.astype(bf16)
    dense_part[...] = dot_first(mixed, seed_low).astype(bf16).reshape(dense_part.shape)

    d_mixed = dot_last(seed_low, w_out[...]).astype(bf16).astype(f32)
    grad[:, :width] = (d_mixed * mid * (gate_sig * (1.0 + gate_in * (1.0 - gate_sig)))).astype(bf16)
    d_att = centre_back(d_mixed * gate, mid, mid_spread).astype(bf16)

    def keep(part, h, value):
        cols = columns(part, h)
        x = before[:, cols]
        sig = jax.nn.sigmoid(x)
        grad[:, cols] = (value * (sig * (1.0 + x * (1.0 - sig)))).astype(bf16)

    for h in range(HEADS):
        weights, slope = kept[h]
        d_head = d_att[:, h * head : (h + 1) * head]
        d_scores = (dot_last(d_head, after[:, columns(1, h)]) * slope * scale).astype(bf16)
        keep(1, h, dot_first(weights, d_head))
        keep(2, h, dot_plain(d_scores, after[:, columns(3, h)]))
        keep(3, h, dot_first(d_scores, after[:, columns(2, h)]))
    d_normed = dot_last(grad[:, :width], w_in[:, :width])
    for b in range(1, 4):
        cols = slice(b * width, (b + 1) * width)
        d_normed = d_normed + dot_last(grad[:, cols], w_in[:, cols])
    row_grad = (centre_back(d_normed, unit, spread) + seed).astype(bf16)
    nz, cap, _ = outgoing.shape
    spots = hot((nz * cap, span), position[...])
    outgoing[...] = dot_plain(spots, row_grad).astype(bf16).reshape(outgoing.shape)


def step_kernel(
    scale,
    lengths,
    table_far,
    owners,
    rows,
    w_in_far,
    w_out_far,
    cotangent_far,
    table_out,
    dense_out,
    table,
    w_in,
    w_out,
    cotangent,
    near_s,
    embedded,
    position,
    incoming,
    outgoing,
    dense_part,
    *scratch,
):
    nz = outgoing.shape[0]
    me = lax.axis_index("table")
    spot = lax.axis_index("dp")
    x = spot // NY
    y = lax.rem(spot, NY)
    barrier = pltpu.get_barrier_semaphore()

    def greet(axis, peer):
        pl.semaphore_signal(barrier, inc=1, device_id={axis: peer}, device_id_type=MESH)

    each(1, nz, lambda k: greet("table", lax.rem(me + k, nz)))
    each(1, NX, lambda k: greet("dp", lax.rem(x + k, NX) * NY + y))
    each(1, NY, lambda k: greet("dp", x * NY + lax.rem(y + k, NY)))

    pairs = ((table_far, table), (w_in_far, w_in), (w_out_far, w_out), (cotangent_far, cotangent))
    copies = [pltpu.make_async_copy(a, b, near_s.at[i]) for i, (a, b) in enumerate(pairs)]
    for copy in copies:
        copy.start()

    def ready():
        pl.semaphore_wait(barrier, nz - 1 + NX - 1 + NY - 1)

    fetch_kernel(
        ready, copies[0].wait, table, owners, rows, embedded, position, incoming, *scratch[:8]
    )
    for copy in copies[1:]:
        copy.wait()
    layer_kernel(
        lengths,
        embedded,
        position,
        w_in,
        w_out,
        cotangent,
        outgoing,
        dense_part,
        *scratch[8:11],
    )
    exchange_kernel(
        scale, outgoing, dense_part, incoming, table_out, dense_out, *scratch[11:]
    )


def step(lengths, table, owners, rows, w_in, w_out, cotangent, groups, capacity, scale):
    shard_rows, width = table.shape
    slots = owners.shape[1]
    bf16, f32, i32 = jnp.bfloat16, jnp.float32, jnp.int32
    piece = (shard_rows // NX // 2, 128)
    small = (capacity, 128)
    block = (groups, capacity, width)
    vmem = pl.BlockSpec(memory_space=pltpu.VMEM)
    far = pl.BlockSpec(memory_space=pl.ANY)
    dma = pltpu.SemaphoreType.DMA
    room = pltpu.VMEM

    def pair(*dims):
        return [dma(dims), dma(dims)]

    return pl.pallas_call(
        functools.partial(step_kernel, scale),
        out_shape=(
            jax.ShapeDtypeStruct((shard_rows, width), bf16),
            jax.ShapeDtypeStruct((groups * capacity, width), bf16),
        ),
        in_specs=[pl.BlockSpec(memory_space=pltpu.SMEM), far, vmem, vmem, far, far, far],
        out_specs=(vmem, vmem),
        scratch_shapes=[
            room(table.shape, bf16),
            room(w_in.shape, bf16),
            room(w_out.shape, bf16),
            room(cotangent.shape, bf16),
            dma((4,)),
            room((slots, width), bf16),
            room((1, slots), i32),
            room((1, groups * capacity), i32),
            room(block, bf16),
            room(block, bf16),
            room((groups, 1, 128), i32),
            room((groups, 1, 128), i32),
            room(block, bf16),
            room(block, bf16),
        ]
        + pair(groups)
        + pair(groups)
        + [
            room((slots, 4 * width), f32),
            room((slots, 4 * width), bf16),
            room((slots, 4 * width), bf16),
            room(block, bf16),
            room((groups // 2,) + small, bf16),
            room((NX, NY) + piece, bf16),
            room((NX, NY) + piece, bf16),
            room((NY,) + piece, bf16),
            room((NY,) + piece, bf16),
            room((NX, NY) + piece, bf16),
            room((NX, groups // 2) + small, bf16),
            room((NX, groups // 2) + small, bf16),
            room((NY,) + small, bf16),
            room((NX,) + small, bf16),
            room((groups, NX) + small, bf16),
        ]
        + pair(groups)
        + pair(groups)
        + pair(NX, NY)
        + pair(NY)
        + pair(NY)
        + pair(NX, NY)
        + pair(NX)
        + pair(NY)
        + pair(NX)
        + pair(groups)
        + pair(groups // 2)
        + [
            dma((groups,)),
            room((NY,) + piece, bf16),
            room((groups // 2, capacity, width), bf16),
            room((groups // 2, capacity, width), bf16),
            room((groups // 2,) + small, bf16),
        ],
        compiler_params=pltpu.CompilerParams(
            collective_id=0, has_side_effects=True, vmem_limit_bytes=60 << 20
        ),
    )(lengths, table, owners, rows, w_in, w_out, cotangent)


def per_device(table, history_shard, history_row, lengths, w_in, w_out, cotangent):
    shard_rows, model_width = table.shape
    samples_here, seq_span = history_row.shape
    groups = lax.axis_size("table")
    copies = lax.axis_size("dp")
    slot_count = samples_here * seq_span
    capacity = 2 * slot_count // groups
    total_slots = slot_count * copies * groups
    grad_scale = 1.0 / math.sqrt(total_slots)
    table_sum, dense_grad = step(
        lengths,
        table,
        history_shard.reshape(1, slot_count),
        history_row.reshape(1, slot_count),
        w_in,
        w_out,
        cotangent.reshape(slot_count, model_width),
        groups,
        capacity,
        grad_scale,
    )
    table_grad = table_sum.astype(jnp.float32)
    return (table_grad, dense_grad)


def solution(mesh):
    in_specs = (
        P("table", None),
        P(("dp", "table"), None, None),
        P(("dp", "table"), None),
        P(("dp", "table")),
        P(),
        P(),
        P(("dp", "table"), None, None),
    )
    out_specs = (P("table", None), P())
    return jax.shard_map(
        per_device, mesh=mesh, in_specs=in_specs, out_specs=out_specs, check_vma=False
    )
```
